32 devices in a mesh: ccd: 4 (over z), tile: 8 (over y, x, core).
Axes of the slice: x: 2, y: 2, z: 4, core: 2. Of those that a mesh axis runs over, the one named last changes fastest.
Arguments:
- frames: bfloat16 [256, 512, 128], P(None, ('ccd', 'tile')), may hold values from -24 to 24
- source_mask: int32 [256, 512, 128], P(None, ('ccd', 'tile')), may hold values 0 or 1
- good_pixels: int32 [512, 128], P(('ccd', 'tile')), may hold values 0 or 1
Outputs:
- factor: float32 [256, 256], replicated
- basis: bfloat16 [256, 512, 128], P(None, ('ccd', 'tile'))
The draws below stay inside these ranges and needn't reach their ends.
All inputs are finite; a program needn't handle non-finite values. No bound on the sum of `source_mask` or of `good_pixels` on one device may be relied on, other than what follows from the above.
Results may differ from the reference program's by a relative error of at most 0.00065.
Values may be sent and summed in bfloat16 or wider, within the bound.
A program may use at most 64 MiB of HBM per device.

```python
import math
import jax
import jax.numpy as jnp
from jax import lax

EXPOSURES = 256
REACH = 16
TILE_COLS = 128
CCDS = 2
ROWS = 256
ALL_ROWS = 512
PIXELS = 65536


def draw_frames(key, part):
    keys = jax.random.split(jax.random.fold_in(key, 11), 3)
    shape = (EXPOSURES, ALL_ROWS, TILE_COLS)
    base = jax.random.normal(keys[0], shape, jnp.float32)
    exposure_scale = 0.3 * jnp.exp(jax.random.uniform(keys[1], (EXPOSURES, 1, 1), jnp.float32, 0.0, math.log(10.0)))
    pixel_scale = jnp.exp(jax.random.uniform(keys[2], (1, ALL_ROWS, TILE_COLS), jnp.float32, math.log(0.3), math.log(3.0)))
    values = base * exposure_scale * pixel_scale
    return jnp.clip(values, -24.0, 24.0).astype(jnp.bfloat16)


def plant(drawn, stream_key, low, largest):
    extent = drawn.shape
    spot = [jax.random.randint(jax.random.fold_in(stream_key, axis), (), 0, extent[axis]) for axis in range(len(extent))]
    drawn = drawn.at[tuple(spot)].set(low)
    longest = extent.index(max(extent))
    spot[longest] = (spot[longest] + 1) % extent[longest]
    return drawn.at[tuple(spot)].set(largest)


def setup_inputs(seed: int = 0) -> dict:
    key_list = jax.random.split(jax.random.key(seed), 4)
    frames = draw_frames(jax.random.fold_in(key_list[3], 71), 0)
    source_mask = plant((jax.random.randint(key_list[1], (EXPOSURES, ALL_ROWS, TILE_COLS), 0, 8) < 7).astype(jnp.int32), jax.random.fold_in(key_list[1], 1), 0, 1)
    good_pixels = plant((jax.random.randint(key_list[2], (ALL_ROWS, TILE_COLS), 0, 16) < 15).astype(jnp.int32), jax.random.fold_in(key_list[2], 1), 0, 1)
    return dict(frames=frames, source_mask=source_mask, good_pixels=good_pixels)


def kernel_taps():
    offsets = jnp.arange(-REACH, REACH + 1).astype(jnp.float32)
    raw = jnp.exp(-jnp.abs(offsets) / 6.0)
    return raw / jnp.sqrt(jnp.sum(raw * raw))

def smooth_ccd(frames, source_mask, good_pixels, index):
    start = (index * ROWS).astype(jnp.int32)
    row_ids = start - REACH + jnp.arange(ROWS + 2 * REACH).astype(jnp.int32)
    valid = jnp.logical_and(row_ids >= 0, row_ids < ALL_ROWS)
    clipped = jnp.clip(row_ids, 0, ALL_ROWS - 1).astype(jnp.int32)
    valid_f = valid.astype(jnp.float32)
    frame_block = jnp.take(frames, clipped, axis=1).astype(jnp.float32)
    source_block = jnp.take(source_mask, clipped, axis=1).astype(jnp.float32)
    good_block = jnp.take(good_pixels, clipped, axis=0).astype(jnp.float32)[None]
    padded = frame_block * source_block * good_block * valid_f.reshape(1, ROWS + 2 * REACH, 1)
    taps = kernel_taps()
    rows_done = jnp.zeros((EXPOSURES, ROWS, TILE_COLS), jnp.float32)
    for offset in range(2 * REACH + 1):
        rows_done = rows_done + taps[offset] * padded[:, offset:offset + ROWS, :]
    padded = jnp.pad(rows_done, ((0, 0), (0, 0), (REACH, REACH)))
    smoothed = jnp.zeros((EXPOSURES, ROWS, TILE_COLS), jnp.float32)
    for offset in range(2 * REACH + 1):
        smoothed = smoothed + taps[offset] * padded[:, :, offset:offset + TILE_COLS]
    return smoothed.reshape(EXPOSURES, ROWS * TILE_COLS)

def reference(frames, source_mask, good_pixels):

    def add_gram(total, index):
        flat = smooth_ccd(frames, source_mask, good_pixels, index)
        part_gram = jnp.einsum('ep,fp->ef', flat, flat, precision=lax.Precision.HIGHEST)
        return (total + part_gram, None)
    indices = jnp.arange(CCDS).astype(jnp.int32)
    gram_sum, _ = lax.scan(add_gram, jnp.zeros((EXPOSURES, EXPOSURES), jnp.float32), indices)
    gram = gram_sum / PIXELS
    lower = jnp.linalg.cholesky(gram)
    factor = lower.T

    def solve_ccd(index):
        flat = smooth_ccd(frames, source_mask, good_pixels, index)
        solved = lax.linalg.triangular_solve(lower, flat, left_side=True, lower=True)
        return solved.astype(jnp.bfloat16).reshape(EXPOSURES, ROWS, TILE_COLS)
    stacked = lax.map(solve_ccd, indices)
    basis = jnp.moveaxis(stacked, 0, 1).reshape(EXPOSURES, ALL_ROWS, TILE_COLS)
    return (factor, basis)
```

```python
import functools
import math

import jax
import jax.numpy as jnp
import numpy as np
from jax import lax
from jax.experimental import pallas as pl
from jax.experimental.pallas import tpu as pltpu
from jax.sharding import PartitionSpec as P

REACH = 16
MESH = pl.DeviceIdType.MESH
HIGH = lax.Precision.HIGHEST
LANES = 128
CHUNKS = 8
GROUPS = 4
AHEAD = 2
VMEM = 60 << 20


def column_matrix(tile_cols):
    distance = np.abs(np.arange(tile_cols)[:, None] - np.arange(tile_cols)[None, :])
    norm = np.sum(np.exp(-2.0 * np.abs(np.arange(-REACH, REACH + 1)) / 6.0))
    full = np.where(distance <= REACH, np.exp(-distance / 6.0) / norm, 0.0).astype(np.float32)
    high = full.astype(jnp.bfloat16)
    low = (full - high.astype(np.float32)).astype(jnp.bfloat16)
    pair = np.concatenate([high, low], axis=1)
    return np.concatenate([pair, pair], axis=0)


def matmul(a, b, contract=(1, 0)):
    return lax.dot_general(
        a, b, (((contract[0],), (contract[1],)), ((), ())), precision=HIGH, preferred_element_type=jnp.float32
    )


def split(value):
    high = value.astype(jnp.bfloat16)
    return high, (value - high.astype(jnp.float32)).astype(jnp.bfloat16)


def product(a, b, contract):
    return lax.dot_general(
        a, b, (((contract[0],), (contract[1],)), ((), ())), preferred_element_type=jnp.float32
    )


def eliminate(block, offset, rows_ref):
    size = block[0].shape[0]
    groups, wide = size // 8, len(block)
    at, start = divmod(offset, LANES)
    full = (8, LANES)
    live = [[tile[8 * g:8 * g + 8, :] for tile in block] for g in range(groups)]
    lane = lax.broadcasted_iota(jnp.int32, full, 1)
    for g in range(groups):
        base = start + 8 * g
        inside = jnp.logical_and(lane >= base, lane < base + 8)
        cols = [jnp.broadcast_to(live[g][at][:, base + k:base + k + 1], full) for k in range(8)]
        small = {(j, k): jnp.broadcast_to(cols[k][j:j + 1, :], full) for j in range(8) for k in range(j, 8)}
        rows = []
        for k in range(8):
            row = [jnp.broadcast_to(tile[k:k + 1, :], full) for tile in live[g]]
            row[at] = jnp.where(inside, jnp.where(lane == base + k, 1.0, 0.0), row[at])
            rows.append(row)
        inv, lower = [], {}
        for j in range(8):
            inv.append(1.0 / small[j, j])
            for k in range(j + 1, 8):
                for m in range(k, 8):
                    small[k, m] = small[k, m] - (small[j, k] * small[j, m]) * inv[j]
            for k in range(j + 1, 8):
                lower[k, j] = small[j, k] * inv[j]
                rows[k] = [x - lower[k, j] * y for x, y in zip(rows[k], rows[j])]
        for j in range(8):
            pivot = small[j, j]
            root = lax.rsqrt(pivot)
            root = root * (1.5 - 0.5 * pivot * root * root)
            out = list(rows[j])
            for m in range(j, 8):
                out[at] = jnp.where(lane == base + m, small[j, m], out[at])
            for w in range(wide):
                rows_ref[8 * g + j:8 * g + j + 1, w * LANES:(w + 1) * LANES] = (out[w] * root)[:1, :]
        if g == groups - 1:
            break
        back = [[x * inv[k] for x in rows[k]] for k in range(8)]
        for k in range(7, -1, -1):
            for m in range(k):
                back[m] = [x - lower[k, m] * y for x, y in zip(back[m], back[k])]
        for i in range(g + 1, groups):
            total = None
            for k in range(8):
                col = jnp.broadcast_to(live[i][at][:, base + k:base + k + 1], full)
                term = [col * y for y in back[k]]
                total = term if total is None else [x + y for x, y in zip(total, term)]
            live[i] = [
                (jnp.where(inside, 0.0, x) if w == at else x) - y for w, (x, y) in enumerate(zip(live[i], total))
            ]


def extend(gram, offset, inverse, lows, rows_ref):
    size = gram[0].shape[0]
    at, start = divmod(offset, LANES)
    wide = at + 1
    shape = (size, LANES)
    lane = lax.broadcasted_iota(jnp.int32, shape, 1)
    row = lax.broadcasted_iota(jnp.int32, shape, 0)
    inside = jnp.logical_and(lane >= start, lane < start + size)
    if offset == 0:
        low = None
        block = [jnp.where(inside, gram[0], 0.0)]
    else:
        value = jnp.concatenate(gram[:wide], axis=1) if wide > 1 else gram[0]
        inv = inverse(wide)
        low = matmul(value, inv, (1, 1))
        lows[offset:offset + size, :wide * LANES] = low
        square = matmul(low, lows[at * LANES:(at + 1) * LANES, :wide * LANES], (1, 1))
        spread = matmul(low, inv)
        block = [-spread[:, w * LANES:(w + 1) * LANES] for w in range(wide)]
        block[at] = jnp.where(inside, gram[at] - square, block[at])
    eliminate(block, offset, rows_ref)
    out, kept = [], []
    for w in range(wide):
        done = rows_ref[:size, w * LANES:(w + 1) * LANES]
        side = None if low is None else low[:, w * LANES:(w + 1) * LANES]
        if w == at:
            upper = jnp.where(lane >= start + row, done, 0.0)
            kept.append(upper if side is None else jnp.where(lane < start, side, upper))
            done = jnp.where(lane < start + row, done, jnp.where(lane == start + row, 1.0 / done, 0.0))
        else:
            kept.append(side)
        out.append(done)
    return out, kept


def smooth_rows(read, rows):
    decay = math.exp(-1.0 / 6.0)
    tail = math.exp(-(REACH + 1) / 6.0)
    ahead = read(0)
    for p in range(1, REACH + 1):
        ahead = ahead * decay + read(p)
    out = [ahead]
    for i in range(1, rows):
        ahead = ahead * decay + (read(REACH + i) - tail * read(i - 1))
        out.append(ahead)
    last = REACH + rows - 1
    back = read(last + REACH) * decay
    for k in range(REACH - 1, 0, -1):
        back = (back + read(last + k)) * decay
    out[rows - 1] = out[rows - 1] + back
    for i in range(rows - 2, -1, -1):
        p = REACH + i
        back = (back + read(p + 1)) * decay - tail * read(p + REACH + 1)
        out[i] = out[i] + back
    return out


def shares(size, tiles, group):
    tall = size * (group * size // LANES + 1)
    return max(8, -(-tall // (8 * tiles)) * 8)


def exchange_kernel(ccds, tiles, pixel_total, frame_hbm, mask_hbm, good_ref, w_ref,
                    hi_hbm, lo_hbm, g_ref, x_ref, f_ref,
                    frames, masks, flat, own, halo, done, hi_ref, lo_ref, lows, rows_ref, *rest):
    bufs = [rest[4 * g:4 * g + 4] for g in range(GROUPS)]
    fs, ms, outs, hs, hr, s1, r1, s2, r2, s3, r3 = rest[4 * GROUPS:]
    exposures, tile_rows, h = frames.shape
    c, t = lax.axis_index("ccd"), lax.axis_index("tile")
    me, total = c * tiles + t, ccds * tiles
    after, before = lax.rem(me + 1, total), lax.rem(me + total - 1, total)
    after_id = (lax.div(after, tiles), lax.rem(after, tiles))
    before_id = (lax.div(before, tiles), lax.rem(before, tiles))
    part = exposures // CHUNKS
    size = exposures // GROUPS
    span = part * tile_rows
    scale = 1.0 / pixel_total
    loads = []
    for k in range(CHUNKS):
        block = pl.ds(k * part, part)
        pair = (pltpu.make_async_copy(frame_hbm.at[block], frames.at[block], fs.at[k]),
                pltpu.make_async_copy(mask_hbm.at[block], masks.at[block], ms.at[k]))
        for copy in pair:
            copy.start()
        loads.append(pair)
    barrier = pltpu.get_barrier_semaphore()
    for peer in (before_id, after_id):
        pl.semaphore_signal(barrier, inc=1, device_id=peer, device_id_type=MESH)
    for d in range(1, tiles):
        pl.semaphore_signal(barrier, inc=1, device_id=(c, lax.rem(t + d, tiles)), device_id_type=MESH)
    for d in range(1, ccds):
        pl.semaphore_signal(barrier, inc=1, device_id=(lax.rem(c + d, ccds), t), device_id_type=MESH)
    good = good_ref[...].astype(jnp.float32)[None]

    def mask(k):
        block = pl.ds(k * part, part)
        for copy in loads[k]:
            copy.wait()
        value = frames[block].astype(jnp.float32) * (masks[block].astype(jnp.float32) * good)
        flat[k % 2] = value.reshape(span, h)
        for r in range(tile_rows):
            own[k, r] = flat[k % 2, pl.ds(r, part, stride=tile_rows), :].astype(jnp.bfloat16)

    moves = []

    def send(k):
        pair = []
        for side, peer in enumerate((after_id, before_id)):
            copy = pltpu.make_async_remote_copy(
                src_ref=own.at[k], dst_ref=halo.at[side, k], send_sem=hs.at[side, k],
                recv_sem=hr.at[side, k], device_id=peer, device_id_type=MESH)
            copy.start()
            pair.append(copy)
        moves.append(pair)

    mask(0)
    pl.semaphore_wait(barrier, tiles + ccds)
    send(0)
    for k in range(1, CHUNKS):
        mask(k)
        if k < AHEAD:
            send(k)
    x_ref[...] = jnp.zeros(x_ref.shape, jnp.float32)
    f_ref[...] = jnp.zeros(f_ref.shape, jnp.float32)
    lows[...] = jnp.zeros(lows.shape, jnp.float32)
    for g in range(GROUPS):
        bufs[g][0][...] = jnp.zeros(bufs[g][0].shape, jnp.float32)
        if (g + 1) * size % LANES and g + 1 < GROUPS:
            for ref in (hi_ref, lo_ref):
                ref[(g + 1) * size:(g + 2) * size, :] = jnp.zeros((size, ref.shape[1]), jnp.bfloat16)
    has_before = jnp.where(me > 0, 1.0, 0.0)
    has_after = jnp.where(me < total - 1, 1.0, 0.0)
    weights = w_ref[...]
    step = 16
    stores = []

    def smooth(k):
        @pl.loop(0, part // step)
        def _(n):
            some = pl.ds(pl.multiple_of(n * step, step), step)

            def read(p):
                if p < tile_rows:
                    return halo[0, k, p, some, :].astype(jnp.float32) * has_before
                if p < 2 * tile_rows:
                    return own[k, p - tile_rows, some, :].astype(jnp.float32)
                return halo[1, k, p - 2 * tile_rows, some, :].astype(jnp.float32) * has_after

            for r, value in enumerate(smooth_rows(read, tile_rows)):
                high, low = split(value)
                where = pl.ds(pl.multiple_of(r * part + n * step, step), step)
                done[where, :h] = high
                done[where, h:] = low

        value = product(done[...], weights, (1, 0))
        high, low = split(value[:, :h] + value[:, h:])
        rows = slice(k * part, (k + 1) * part)
        for r in range(tile_rows):
            hi_ref[rows, r * h:(r + 1) * h] = high[r * part:(r + 1) * part]
            lo_ref[rows, r * h:(r + 1) * h] = low[r * part:(r + 1) * part]
        for i, (src, dst) in enumerate(((hi_ref, hi_hbm), (lo_ref, lo_hbm))):
            copy = pltpu.make_async_copy(src.at[pl.ds(k * part, part)], dst.at[pl.ds(k * part, part)], outs.at[i, k])
            copy.start()
            stores.append(copy)

    sent = []
    waiting = {}

    def launch(g, stage):
        mine, near, far, whole = bufs[g]
        copies = []
        for d in range(1, ccds if stage == 2 else tiles):
            i = d - 1
            if stage == 1:
                peer = lax.rem(t + d, tiles)
                copy = pltpu.make_async_remote_copy(
                    src_ref=mine.at[peer], dst_ref=near.at[i], send_sem=s1.at[g, i], recv_sem=r1.at[g, i],
                    device_id=(c, peer), device_id_type=MESH)
            elif stage == 2:
                copy = pltpu.make_async_remote_copy(
                    src_ref=far.at[c], dst_ref=far.at[c], send_sem=s2.at[g, i], recv_sem=r2.at[g, i],
                    device_id=(lax.rem(c + d, ccds), t), device_id_type=MESH)
            else:
                copy = pltpu.make_async_remote_copy(
                    src_ref=whole.at[t], dst_ref=whole.at[t], send_sem=s3.at[g, i], recv_sem=r3.at[g, i],
                    device_id=(c, lax.rem(t + d, tiles)), device_id_type=MESH)
            copy.start()
            copies.append(copy)
        sent.extend(copies)
        waiting[g] = (stage, copies)

    def gram(g):
        first, stop = g * size, (g + 1) * size
        wide = (first // LANES + 1) * LANES
        some = jnp.concatenate([hi_ref[first:stop, :], lo_ref[first:stop, :]], axis=0)
        value = product(some, hi_ref[:wide, :], (1, 1)) + product(some, lo_ref[:wide, :], (1, 1))
        value = value[:size] + value[size:]
        packed = jnp.concatenate([value[:, w:w + LANES] for w in range(0, wide, LANES)], axis=0)
        mine = bufs[g][0]
        share = mine.shape[1]
        for i in range(packed.shape[0] // share):
            mine[i] = packed[i * share:(i + 1) * share]
        launch(g, 1)

    def advance(g):
        mine, near, far, whole = bufs[g]
        stage, copies = waiting[g]
        for copy in copies:
            copy.wait_recv()
        if stage == 1:
            value = mine[t]
            for d in range(1, tiles):
                value = value + near[d - 1]
            far[c] = value
            launch(g, 2)
        elif stage == 2:
            value = far[0]
            for i in range(1, ccds):
                value = value + far[i]
            whole[t] = value
            launch(g, 3)

    def factor(g):
        whole = bufs[g][3]
        value = whole[...].reshape(-1, LANES) * scale
        tiles_in = [value[w * size:(w + 1) * size] for w in range(g * size // LANES + 1)]
        rows = slice(g * size, (g + 1) * size)
        x, f = extend(tiles_in, g * size, lambda n: x_ref[:n * LANES, :n * LANES], lows, rows_ref)
        for w in range(len(x)):
            x_ref[rows, w * LANES:(w + 1) * LANES] = x[w]
            f_ref[rows, w * LANES:(w + 1) * LANES] = f[w]

    per = CHUNKS // GROUPS
    for k in range(CHUNKS):
        for copy in moves[k]:
            copy.wait_recv()
        if k % per == per - 1:
            for g in range(max(0, k // per - 3), k // per):
                advance(g)
        smooth(k)
        if k % per == per - 1:
            gram(k // per)
        if k + AHEAD < CHUNKS:
            send(k + AHEAD)
    for n in range(3):
        factor(GROUPS - 4 + n)
        for g in range(GROUPS - 1, GROUPS - 4 + n, -1):
            advance(g)
    g_ref[...] = bufs[GROUPS - 1][3][...]
    for copy in stores:
        copy.wait()
    for copy in sum(moves, []) + sent:
        copy.wait_send()


def exchange(frames, source_mask, good_pixels, weights, pixel_total):
    ccds, tiles = lax.axis_size("ccd"), lax.axis_size("tile")
    exposures, tile_rows, _ = frames.shape
    pixels = tile_rows * LANES
    part, size = exposures // CHUNKS, exposures // GROUPS
    span = part * tile_rows
    dma = pltpu.SemaphoreType.DMA
    vm = pl.BlockSpec(memory_space=pltpu.VMEM)
    hbm = pl.BlockSpec(memory_space=pl.ANY)
    split_shape = jax.ShapeDtypeStruct((exposures, pixels), jnp.bfloat16)
    square = jax.ShapeDtypeStruct((exposures, exposures), jnp.float32)
    share = [shares(size, tiles, g) for g in range(GROUPS)]
    reduce = []
    for g in range(GROUPS):
        for n in (tiles, tiles - 1, ccds, tiles):
            reduce.append(pltpu.VMEM((n, share[g], LANES), jnp.float32))
    return pl.pallas_call(
        functools.partial(exchange_kernel, ccds, tiles, pixel_total),
        out_shape=(split_shape, split_shape, jax.ShapeDtypeStruct((tiles, share[-1], LANES), jnp.float32), square, square),
        in_specs=[hbm, hbm, vm, vm],
        out_specs=(hbm, hbm, vm, vm, vm),
        scratch_shapes=[
            pltpu.VMEM(frames.shape, jnp.bfloat16),
            pltpu.VMEM(frames.shape, jnp.int32),
            pltpu.VMEM((2, span, LANES), jnp.float32),
            pltpu.VMEM((CHUNKS, tile_rows, part, LANES), jnp.bfloat16),
            pltpu.VMEM((2, CHUNKS, tile_rows, part, LANES), jnp.bfloat16),
            pltpu.VMEM((span, 2 * LANES), jnp.bfloat16),
            pltpu.VMEM((exposures, pixels), jnp.bfloat16),
            pltpu.VMEM((exposures, pixels), jnp.bfloat16),
            pltpu.VMEM((exposures, exposures), jnp.float32),
            pltpu.VMEM((size, exposures), jnp.float32),
            *reduce,
            dma((CHUNKS,)), dma((CHUNKS,)), dma((2, CHUNKS)),
            dma((2, CHUNKS)), dma((2, CHUNKS)),
            dma((GROUPS, tiles - 1)), dma((GROUPS, tiles - 1)),
            dma((GROUPS, ccds - 1)), dma((GROUPS, ccds - 1)),
            dma((GROUPS, tiles - 1)), dma((GROUPS, tiles - 1)),
        ],
        compiler_params=pltpu.CompilerParams(collective_id=0, has_side_effects=True, vmem_limit_bytes=VMEM),
    )(frames, source_mask, good_pixels, weights)


def solve_kernel(pixel_total, g_ref, x_ref, f_ref, hi_hbm, lo_hbm, o_ref, b_ref,
                 hi_ref, lo_ref, lows, rows_ref, xh_ref, xl_ref, out32, sems):
    loads = (pltpu.make_async_copy(hi_hbm, hi_ref, sems.at[0]), pltpu.make_async_copy(lo_hbm, lo_ref, sems.at[1]))
    for copy in loads:
        copy.start()
    exposures, pixels = hi_ref.shape
    size = exposures // GROUPS
    first = exposures - size
    at = first // LANES
    lows[...] = jnp.zeros(lows.shape, jnp.float32)
    value = g_ref[...].reshape(-1, LANES) * (1.0 / pixel_total)
    block = [value[w * size:(w + 1) * size] for w in range(at + 1)]
    x, f = extend(block, first, lambda n: x_ref[...], lows, rows_ref)
    xh_ref[:first, :], xl_ref[:first, :] = split(x_ref[:first, :])
    xh_ref[first:, :], xl_ref[first:, :] = split(jnp.concatenate(x, axis=1))
    whole = jnp.concatenate([f_ref[:first, :], jnp.concatenate(f, axis=1)], axis=0)
    row = lax.broadcasted_iota(jnp.int32, (exposures, exposures), 0) // size
    col = lax.broadcasted_iota(jnp.int32, (exposures, exposures), 1) // size
    o_ref[...] = jnp.where(row == col, whole, 0.0) + jnp.where(col < row, whole, 0.0).T
    for copy in loads:
        copy.wait()
    tile_rows = pixels // LANES
    for k in range(tile_rows // 2):
        cut = slice(2 * k * LANES, 2 * (k + 1) * LANES)
        hi, lo = hi_ref[:, cut], lo_ref[:, cut]
        part = product(xh_ref[...], hi, (1, 0)) + (
            product(xh_ref[...], lo, (1, 0)) + product(xl_ref[...], hi, (1, 0)) + product(xl_ref[...], lo, (1, 0)))
        for i in range(2):
            out32[pl.ds(2 * k + i, exposures, stride=tile_rows), :] = part[:, i * LANES:(i + 1) * LANES]
    b_ref[...] = out32[...].astype(jnp.bfloat16)


def solve(gram, x, f, hi, lo, pixel_total):
    exposures, pixels = hi.shape
    vm = pl.BlockSpec(memory_space=pltpu.VMEM)
    hbm = pl.BlockSpec(memory_space=pl.ANY)
    square = (exposures, exposures)
    return pl.pallas_call(
        functools.partial(solve_kernel, pixel_total),
        out_shape=(
            jax.ShapeDtypeStruct(square, jnp.float32),
            jax.ShapeDtypeStruct((exposures * pixels // LANES, LANES), jnp.bfloat16),
        ),
        in_specs=[vm, vm, vm, hbm, hbm],
        out_specs=(vm, vm),
        scratch_shapes=[
            pltpu.VMEM((exposures, pixels), jnp.bfloat16),
            pltpu.VMEM((exposures, pixels), jnp.bfloat16),
            pltpu.VMEM(square, jnp.float32),
            pltpu.VMEM((exposures // GROUPS, exposures), jnp.float32),
            pltpu.VMEM(square, jnp.bfloat16),
            pltpu.VMEM(square, jnp.bfloat16),
            pltpu.VMEM((exposures * pixels // LANES, LANES), jnp.float32),
            pltpu.SemaphoreType.DMA((2,)),
        ],
        compiler_params=pltpu.CompilerParams(vmem_limit_bytes=VMEM),
    )(gram, x, f, hi, lo)


def per_device(frames, source_mask, good_pixels):
    exposures, tile_rows, tile_cols = frames.shape
    tiles = lax.axis_size("tile")
    pixel_total = float(tile_rows * tile_cols * lax.axis_size("ccd") * tiles)
    hi, lo, gram, x, f = exchange(frames, source_mask, good_pixels, column_matrix(tile_cols), pixel_total)
    factor, basis = solve(gram, x, f, hi, lo, pixel_total)
    return (factor, basis.reshape(exposures, tile_rows, tile_cols))


def solution(mesh):
    in_specs = (
        P(None, ("ccd", "tile"), None),
        P(None, ("ccd", "tile"), None),
        P(("ccd", "tile"), None),
    )
    out_specs = (P(), P(None, ("ccd", "tile"), None))
    return jax.shard_map(
        per_device, mesh=mesh, in_specs=in_specs, out_specs=out_specs, check_vma=False
    )
```

```python
import functools
import math

import jax
import jax.numpy as jnp
import numpy as np
from jax import lax
from jax.experimental import pallas as pl
from jax.experimental.pallas import tpu as pltpu
from jax.sharding import PartitionSpec as P

REACH = 16
MESH = pl.DeviceIdType.MESH
HIGH = lax.Precision.HIGHEST
LANES = 128
CHUNKS = 8
GROUPS = 4
AHEAD = 2
VMEM = 40 << 20


def column_matrix(tile_cols):
    distance = np.abs(np.arange(tile_cols)[:, None] - np.arange(tile_cols)[None, :])
    norm = np.sum(np.exp(-2.0 * np.abs(np.arange(-REACH, REACH + 1)) / 6.0))
    full = np.where(distance <= REACH, np.exp(-distance / 6.0) / norm, 0.0).astype(np.float32)
    high = full.astype(jnp.bfloat16)
    low = (full - high.astype(np.float32)).astype(jnp.bfloat16)
    pair = np.concatenate([high, low], axis=1)
    return np.concatenate([pair, pair], axis=0)


def matmul(a, b, contract=(1, 0)):
    return lax.dot_general(
        a, b, (((contract[0],), (contract[1],)), ((), ())), precision=HIGH, preferred_element_type=jnp.float32
    )


def split(value):
    high = value.astype(jnp.bfloat16)
    return high, (value - high.astype(jnp.float32)).astype(jnp.bfloat16)


def product(a, b, contract):
    return lax.dot_general(
        a, b, (((contract[0],), (contract[1],)), ((), ())), preferred_element_type=jnp.float32
    )


def eliminate(block, offset, rows_ref):
    size = block[0].shape[0]
    groups, wide = size // 8, len(block)
    at, start = divmod(offset, LANES)
    full = (8, LANES)
    live = [[tile[8 * g:8 * g + 8, :] for tile in block] for g in range(groups)]
    lane = lax.broadcasted_iota(jnp.int32, full, 1)
    for g in range(groups):
        base = start + 8 * g
        inside = jnp.logical_and(lane >= base, lane < base + 8)
        cols = [jnp.broadcast_to(live[g][at][:, base + k:base + k + 1], full) for k in range(8)]
        small = {(j, k): jnp.broadcast_to(cols[k][j:j + 1, :], full) for j in range(8) for k in range(j, 8)}
        rows = []
        for k in range(8):
            row = [jnp.broadcast_to(tile[k:k + 1, :], full) for tile in live[g]]
            row[at] = jnp.where(inside, jnp.where(lane == base + k, 1.0, 0.0), row[at])
            rows.append(row)
        inv, lower = [], {}
        for j in range(8):
            inv.append(1.0 / small[j, j])
            for k in range(j + 1, 8):
                for m in range(k, 8):
                    small[k, m] = small[k, m] - (small[j, k] * small[j, m]) * inv[j]
            for k in range(j + 1, 8):
                lower[k, j] = small[j, k] * inv[j]
                rows[k] = [x - lower[k, j] * y for x, y in zip(rows[k], rows[j])]
        for j in range(8):
            pivot = small[j, j]
            root = lax.rsqrt(pivot)
            root = root * (1.5 - 0.5 * pivot * root * root)
            out = list(rows[j])
            for m in range(j, 8):
                out[at] = jnp.where(lane == base + m, small[j, m], out[at])
            for w in range(wide):
                rows_ref[8 * g + j:8 * g + j + 1, w * LANES:(w + 1) * LANES] = (out[w] * root)[:1, :]
        if g == groups - 1:
            break
        back = [[x * inv[k] for x in rows[k]] for k in range(8)]
        for k in range(7, -1, -1):
            for m in range(k):
                back[m] = [x - lower[k, m] * y for x, y in zip(back[m], back[k])]
        for i in range(g + 1, groups):
            total = None
            for k in range(8):
                col = jnp.broadcast_to(live[i][at][:, base + k:base + k + 1], full)
                term = [col * y for y in back[k]]
                total = term if total is None else [x + y for x, y in zip(total, term)]
            live[i] = [
                (jnp.where(inside, 0.0, x) if w == at else x) - y for w, (x, y) in enumerate(zip(live[i], total))
            ]


def extend(gram, offset, inverse, lows, rows_ref):
    size = gram[0].shape[0]
    at, start = divmod(offset, LANES)
    wide = at + 1
    shape = (size, LANES)
    lane = lax.broadcasted_iota(jnp.int32, shape, 1)
    row = lax.broadcasted_iota(jnp.int32, shape, 0)
    inside = jnp.logical_and(lane >= start, lane < start + size)
    if offset == 0:
        low = None
        block = [jnp.where(inside, gram[0], 0.0)]
    else:
        value = jnp.concatenate(gram[:wide], axis=1) if wide > 1 else gram[0]
        inv = inverse(wide)
        low = matmul(value, inv, (1, 1))
        lows[offset:offset + size, :wide * LANES] = low
        square = matmul(low, lows[at * LANES:(at + 1) * LANES, :wide * LANES], (1, 1))
        spread = matmul(low, inv)
        block = [-spread[:, w * LANES:(w + 1) * LANES] for w in range(wide)]
        block[at] = jnp.where(inside, gram[at] - square, block[at])
    eliminate(block, offset, rows_ref)
    out, kept = [], []
    for w in range(wide):
        done = rows_ref[:size, w * LANES:(w + 1) * LANES]
        side = None if low is None else low[:, w * LANES:(w + 1) * LANES]
        if w == at:
            upper = jnp.where(lane >= start + row, done, 0.0)
            kept.append(upper if side is None else jnp.where(lane < start, side, upper))
            done = jnp.where(lane < start + row, done, jnp.where(lane == start + row, 1.0 / done, 0.0))
        else:
            kept.append(side)
        out.append(done)
    return out, kept


def smooth_rows(read, rows):
    decay = math.exp(-1.0 / 6.0)
    tail = math.exp(-(REACH + 1) / 6.0)
    ahead = read(0)
    for p in range(1, REACH + 1):
        ahead = ahead * decay + read(p)
    out = [ahead]
    for i in range(1, rows):
        ahead = ahead * decay + (read(REACH + i) - tail * read(i - 1))
        out.append(ahead)
    last = REACH + rows - 1
    back = read(last + REACH) * decay
    for k in range(REACH - 1, 0, -1):
        back = (back + read(last + k)) * decay
    out[rows - 1] = out[rows - 1] + back
    for i in range(rows - 2, -1, -1):
        p = REACH + i
        back = (back + read(p + 1)) * decay - tail * read(p + REACH + 1)
        out[i] = out[i] + back
    return out


def shares(size, tiles, group):
    tall = size * (group * size // LANES + 1)
    return max(8, -(-tall // (8 * tiles)) * 8)


def exchange_kernel(ccds, tiles, pixel_total, frame_hbm, mask_hbm, good_hbm, w_hbm,
                    hi_ref, lo_ref, g_ref, x_ref, f_ref,
                    good_ref, w_ref, frames, masks, flat, own, halo, done, lows, rows_ref, *rest):
    bufs = [rest[4 * g:4 * g + 4] for g in range(GROUPS)]
    fs, ms, ws, hs, hr, s1, r1, s2, r2, s3, r3 = rest[4 * GROUPS:]
    exposures, tile_rows, h = frames.shape
    c, t = lax.axis_index("ccd"), lax.axis_index("tile")
    me, total = c * tiles + t, ccds * tiles
    after, before = lax.rem(me + 1, total), lax.rem(me + total - 1, total)
    after_id = (lax.div(after, tiles), lax.rem(after, tiles))
    before_id = (lax.div(before, tiles), lax.rem(before, tiles))
    part = exposures // CHUNKS
    size = exposures // GROUPS
    span = part * tile_rows
    scale = 1.0 / pixel_total
    loads = []
    small = [pltpu.make_async_copy(good_hbm, good_ref, ws.at[0]), pltpu.make_async_copy(w_hbm, w_ref, ws.at[1])]
    small[0].start()
    for k in range(CHUNKS):
        block = pl.ds(k * part, part)
        pair = (pltpu.make_async_copy(frame_hbm.at[block], frames.at[block], fs.at[k]),
                pltpu.make_async_copy(mask_hbm.at[block], masks.at[block], ms.at[k]))
        for copy in pair:
            copy.start()
        loads.append(pair)
    small[1].start()
    barrier = pltpu.get_barrier_semaphore()
    for peer in (before_id, after_id):
        pl.semaphore_signal(barrier, inc=1, device_id=peer, device_id_type=MESH)
    for d in range(1, tiles):
        pl.semaphore_signal(barrier, inc=1, device_id=(c, lax.rem(t + d, tiles)), device_id_type=MESH)
    for d in range(1, ccds):
        pl.semaphore_signal(barrier, inc=1, device_id=(lax.rem(c + d, ccds), t), device_id_type=MESH)
    small[0].wait()
    good = good_ref[...].astype(jnp.float32)[None]

    def mask(k):
        block = pl.ds(k * part, part)
        for copy in loads[k]:
            copy.wait()
        value = frames[block].astype(jnp.float32) * (masks[block].astype(jnp.float32) * good)
        flat[k % 2] = value.reshape(span, h)
        for r in range(tile_rows):
            own[k, r] = flat[k % 2, pl.ds(r, part, stride=tile_rows), :].astype(jnp.bfloat16)

    moves = []

    def send(k):
        pair = []
        for side, peer in enumerate((after_id, before_id)):
            copy = pltpu.make_async_remote_copy(
                src_ref=own.at[k], dst_ref=halo.at[side, k], send_sem=hs.at[side, k],
                recv_sem=hr.at[side, k], device_id=peer, device_id_type=MESH)
            copy.start()
            pair.append(copy)
        moves.append(pair)

    mask(0)
    pl.semaphore_wait(barrier, tiles + ccds)
    send(0)
    for k in range(1, CHUNKS):
        mask(k)
        if k < AHEAD:
            send(k)
    x_ref[...] = jnp.zeros(x_ref.shape, jnp.float32)
    f_ref[...] = jnp.zeros(f_ref.shape, jnp.float32)
    lows[...] = jnp.zeros(lows.shape, jnp.float32)
    for g in range(GROUPS):
        bufs[g][0][...] = jnp.zeros(bufs[g][0].shape, jnp.float32)
        if (g + 1) * size % LANES and g + 1 < GROUPS:
            for ref in (hi_ref, lo_ref):
                ref[(g + 1) * size:(g + 2) * size, :] = jnp.zeros((size, ref.shape[1]), jnp.bfloat16)
    has_before = jnp.where(me > 0, 1.0, 0.0)
    has_after = jnp.where(me < total - 1, 1.0, 0.0)
    small[1].wait()
    weights = w_ref[...]
    step = 16

    def smooth(k):
        @pl.loop(0, part // step)
        def _(n):
            some = pl.ds(pl.multiple_of(n * step, step), step)

            def read(p):
                if p < tile_rows:
                    return halo[0, k, p, some, :].astype(jnp.float32) * has_before
                if p < 2 * tile_rows:
                    return own[k, p - tile_rows, some, :].astype(jnp.float32)
                return halo[1, k, p - 2 * tile_rows, some, :].astype(jnp.float32) * has_after

            for r, value in enumerate(smooth_rows(read, tile_rows)):
                high, low = split(value)
                where = pl.ds(pl.multiple_of(r * part + n * step, step), step)
                done[where, :h] = high
                done[where, h:] = low

        value = product(done[...], weights, (1, 0))
        high, low = split(value[:, :h] + value[:, h:])
        rows = slice(k * part, (k + 1) * part)
        for r in range(tile_rows):
            hi_ref[rows, r * h:(r + 1) * h] = high[r * part:(r + 1) * part]
            lo_ref[rows, r * h:(r + 1) * h] = low[r * part:(r + 1) * part]

    sent = []
    waiting = {}

    def launch(g, stage):
        mine, near, far, whole = bufs[g]
        copies = []
        for d in range(1, ccds if stage == 2 else tiles):
            i = d - 1
            if stage == 1:
                peer = lax.rem(t + d, tiles)
                copy = pltpu.make_async_remote_copy(
                    src_ref=mine.at[peer], dst_ref=near.at[i], send_sem=s1.at[g, i], recv_sem=r1.at[g, i],
                    device_id=(c, peer), device_id_type=MESH)
            elif stage == 2:
                copy = pltpu.make_async_remote_copy(
                    src_ref=far.at[c], dst_ref=far.at[c], send_sem=s2.at[g, i], recv_sem=r2.at[g, i],
                    device_id=(lax.rem(c + d, ccds), t), device_id_type=MESH)
            else:
                copy = pltpu.make_async_remote_copy(
                    src_ref=whole.at[t], dst_ref=whole.at[t], send_sem=s3.at[g, i], recv_sem=r3.at[g, i],
                    device_id=(c, lax.rem(t + d, tiles)), device_id_type=MESH)
            copy.start()
            copies.append(copy)
        sent.extend(copies)
        waiting[g] = (stage, copies)

    def gram(g):
        first, stop = g * size, (g + 1) * size
        wide = (first // LANES + 1) * LANES
        some = jnp.concatenate([hi_ref[first:stop, :], lo_ref[first:stop, :]], axis=0)
        value = product(some, hi_ref[:wide, :], (1, 1)) + product(some, lo_ref[:wide, :], (1, 1))
        value = value[:size] + value[size:]
        packed = jnp.concatenate([value[:, w:w + LANES] for w in range(0, wide, LANES)], axis=0)
        mine = bufs[g][0]
        share = mine.shape[1]
        for i in range(packed.shape[0] // share):
            mine[i] = packed[i * share:(i + 1) * share]
        launch(g, 1)

    def advance(g):
        mine, near, far, whole = bufs[g]
        stage, copies = waiting[g]
        for copy in copies:
            copy.wait_recv()
        if stage == 1:
            value = mine[t]
            for d in range(1, tiles):
                value = value + near[d - 1]
            far[c] = value
            launch(g, 2)
        elif stage == 2:
            value = far[0]
            for i in range(1, ccds):
                value = value + far[i]
            whole[t] = value
            launch(g, 3)

    def factor(g):
        whole = bufs[g][3]
        value = whole[...].reshape(-1, LANES) * scale
        tiles_in = [value[w * size:(w + 1) * size] for w in range(g * size // LANES + 1)]
        rows = slice(g * size, (g + 1) * size)
        x, f = extend(tiles_in, g * size, lambda n: x_ref[:n * LANES, :n * LANES], lows, rows_ref)
        for w in range(len(x)):
            x_ref[rows, w * LANES:(w + 1) * LANES] = x[w]
            f_ref[rows, w * LANES:(w + 1) * LANES] = f[w]

    per = CHUNKS // GROUPS
    for k in range(CHUNKS):
        for copy in moves[k]:
            copy.wait_recv()
        if k % per == per - 1:
            for g in range(max(0, k // per - 3), k // per):
                advance(g)
        smooth(k)
        if k % per == per - 1:
            gram(k // per)
        if k + AHEAD < CHUNKS:
            send(k + AHEAD)
    for n in range(3):
        factor(GROUPS - 4 + n)
        for g in range(GROUPS - 1, GROUPS - 4 + n, -1):
            advance(g)
    g_ref[...] = bufs[GROUPS - 1][3][...]
    for copy in sum(moves, []) + sent:
        copy.wait_send()


def exchange(frames, source_mask, good_pixels, weights, pixel_total):
    ccds, tiles = lax.axis_size("ccd"), lax.axis_size("tile")
    exposures, tile_rows, _ = frames.shape
    pixels = tile_rows * LANES
    part, size = exposures // CHUNKS, exposures // GROUPS
    span = part * tile_rows
    dma = pltpu.SemaphoreType.DMA
    vm = pl.BlockSpec(memory_space=pltpu.VMEM)
    hbm = pl.BlockSpec(memory_space=pl.ANY)
    split_shape = pltpu.VMEM((exposures, pixels), jnp.bfloat16)
    square = pltpu.VMEM((exposures, exposures), jnp.float32)
    share = [shares(size, tiles, g) for g in range(GROUPS)]
    reduce = []
    for g in range(GROUPS):
        for n in (tiles, tiles - 1, ccds, tiles):
            reduce.append(pltpu.VMEM((n, share[g], LANES), jnp.float32))
    return pl.pallas_call(
        functools.partial(exchange_kernel, ccds, tiles, pixel_total),
        out_shape=(split_shape, split_shape, pltpu.VMEM((tiles, share[-1], LANES), jnp.float32), square, square),
        in_specs=[hbm] * 4,
        out_specs=(vm,) * 5,
        scratch_shapes=[
            pltpu.VMEM(good_pixels.shape, jnp.int32),
            pltpu.VMEM(weights.shape, jnp.bfloat16),
            pltpu.VMEM(frames.shape, jnp.bfloat16),
            pltpu.VMEM(frames.shape, jnp.int32),
            pltpu.VMEM((2, span, LANES), jnp.float32),
            pltpu.VMEM((CHUNKS, tile_rows, part, LANES), jnp.bfloat16),
            pltpu.VMEM((2, CHUNKS, tile_rows, part, LANES), jnp.bfloat16),
            pltpu.VMEM((span, 2 * LANES), jnp.bfloat16),
            pltpu.VMEM((exposures, exposures), jnp.float32),
            pltpu.VMEM((size, exposures), jnp.float32),
            *reduce,
            dma((CHUNKS,)), dma((CHUNKS,)), dma((2,)),
            dma((2, CHUNKS)), dma((2, CHUNKS)),
            dma((GROUPS, tiles - 1)), dma((GROUPS, tiles - 1)),
            dma((GROUPS, ccds - 1)), dma((GROUPS, ccds - 1)),
            dma((GROUPS, tiles - 1)), dma((GROUPS, tiles - 1)),
        ],
        compiler_params=pltpu.CompilerParams(collective_id=0, has_side_effects=True, vmem_limit_bytes=VMEM),
    )(*(pltpu.with_memory_space_constraint(x, pltpu.HBM) for x in (frames, source_mask, good_pixels, weights)))


def solve_kernel(pixel_total, g_ref, x_ref, f_ref, hi_ref, lo_ref, o_ref, b_hbm,
                 lows, rows_ref, out32, packed, sems):
    exposures, pixels = hi_ref.shape
    tile_rows = pixels // LANES
    size = exposures // GROUPS
    first = exposures - size
    at = first // LANES
    copies = []

    def basis(start, x):
        tall = x.shape[0]
        both = jnp.concatenate(split(x), axis=0)
        for k in range(tile_rows // 2):
            cut = slice(2 * k * LANES, 2 * (k + 1) * LANES)
            value = product(both, hi_ref[:, cut], (1, 0)) + product(both, lo_ref[:, cut], (1, 0))
            value = value[:tall] + value[tall:]
            for i in range(2):
                out32[pl.ds(start * tile_rows + 2 * k + i, tall, stride=tile_rows), :] = value[:, i * LANES:(i + 1) * LANES]
        rows = pl.ds(start * tile_rows, tall * tile_rows)
        packed[rows, :] = out32[rows, :].astype(jnp.bfloat16)
        copy = pltpu.make_async_copy(packed.at[rows], b_hbm.at[rows], sems.at[len(copies)])
        copy.start()
        copies.append(copy)

    basis(0, x_ref[:first, :])
    lows[...] = jnp.zeros(lows.shape, jnp.float32)
    value = g_ref[...].reshape(-1, LANES) * (1.0 / pixel_total)
    block = [value[w * size:(w + 1) * size] for w in range(at + 1)]
    x, f = extend(block, first, lambda n: x_ref[...], lows, rows_ref)
    basis(first, jnp.concatenate(x, axis=1))
    whole = jnp.concatenate([f_ref[:first, :], jnp.concatenate(f, axis=1)], axis=0)
    row = lax.broadcasted_iota(jnp.int32, (exposures, exposures), 0) // size
    col = lax.broadcasted_iota(jnp.int32, (exposures, exposures), 1) // size
    o_ref[...] = jnp.where(row == col, whole, 0.0) + jnp.where(col < row, whole, 0.0).T
    for copy in copies:
        copy.wait()


def solve(gram, x, f, hi, lo, pixel_total):
    exposures, pixels = hi.shape
    vm = pl.BlockSpec(memory_space=pltpu.VMEM)
    square = (exposures, exposures)
    rows = (exposures * pixels // LANES, LANES)
    given = (pltpu.with_memory_space_constraint(value, pltpu.VMEM) for value in (gram, x, f, hi, lo))
    return pl.pallas_call(
        functools.partial(solve_kernel, pixel_total),
        out_shape=(jax.ShapeDtypeStruct(square, jnp.float32), jax.ShapeDtypeStruct(rows, jnp.bfloat16)),
        in_specs=[vm] * 5,
        out_specs=(vm, pl.BlockSpec(memory_space=pl.ANY)),
        scratch_shapes=[
            pltpu.VMEM(square, jnp.float32),
            pltpu.VMEM((exposures // GROUPS, exposures), jnp.float32),
            pltpu.VMEM(rows, jnp.float32),
            pltpu.VMEM(rows, jnp.bfloat16),
            pltpu.SemaphoreType.DMA((2,)),
        ],
        compiler_params=pltpu.CompilerParams(vmem_limit_bytes=VMEM),
    )(*given)


def per_device(frames, source_mask, good_pixels):
    exposures, tile_rows, tile_cols = frames.shape
    tiles = lax.axis_size("tile")
    pixel_total = float(tile_rows * tile_cols * lax.axis_size("ccd") * tiles)
    hi, lo, gram, x, f = exchange(frames, source_mask, good_pixels, column_matrix(tile_cols), pixel_total)
    factor, basis = solve(gram, x, f, hi, lo, pixel_total)
    return (factor, basis.reshape(exposures, tile_rows, tile_cols))


def solution(mesh):
    in_specs = (
        P(None, ("ccd", "tile"), None),
        P(None, ("ccd", "tile"), None),
        P(("ccd", "tile"), None),
    )
    out_specs = (P(), P(None, ("ccd", "tile"), None))
    return jax.shard_map(
        per_device, mesh=mesh, in_specs=in_specs, out_specs=out_specs, check_vma=False
    )
```

```python
import functools
import math

import jax
import jax.numpy as jnp
import numpy as np
from jax import lax
from jax.experimental import pallas as pl
from jax.experimental.pallas import tpu as pltpu
from jax.sharding import PartitionSpec as P

REACH = 16
MESH = pl.DeviceIdType.MESH
HIGH = lax.Precision.HIGHEST
LANES = 128
CHUNKS = 8
GROUPS = 4
AHEAD = 2
VMEM = 40 << 20


def column_matrix(tile_cols):
    distance = np.abs(np.arange(tile_cols)[:, None] - np.arange(tile_cols)[None, :])
    norm = np.sum(np.exp(-2.0 * np.abs(np.arange(-REACH, REACH + 1)) / 6.0))
    full = np.where(distance <= REACH, np.exp(-distance / 6.0) / norm, 0.0).astype(np.float32)
    high = full.astype(jnp.bfloat16)
    low = (full - high.astype(np.float32)).astype(jnp.bfloat16)
    pair = np.concatenate([high, low], axis=1)
    return np.concatenate([pair, pair], axis=0)


def matmul(a, b, contract=(1, 0)):
    return lax.dot_general(
        a, b, (((contract[0],), (contract[1],)), ((), ())), precision=HIGH, preferred_element_type=jnp.float32
    )


def split(value):
    high = value.astype(jnp.bfloat16)
    return high, (value - high.astype(jnp.float32)).astype(jnp.bfloat16)


def product(a, b, contract):
    return lax.dot_general(
        a, b, (((contract[0],), (contract[1],)), ((), ())), preferred_element_type=jnp.float32
    )


def eliminate(block, offset, rows_ref, fill=()):
    size = block[0].shape[0]
    groups, wide = size // 8, len(block)
    at, start = divmod(offset, LANES)
    full = (8, LANES)
    live = [[tile[8 * g:8 * g + 8, :] for tile in block] for g in range(groups)]
    lane = lax.broadcasted_iota(jnp.int32, full, 1)
    for g in range(groups):
        base = start + 8 * g
        inside = jnp.logical_and(lane >= base, lane < base + 8)
        cols = [jnp.broadcast_to(live[g][at][:, base + k:base + k + 1], full) for k in range(8)]
        small = {(j, k): jnp.broadcast_to(cols[k][j:j + 1, :], full) for j in range(8) for k in range(j, 8)}
        rows = []
        for k in range(8):
            row = [jnp.broadcast_to(tile[k:k + 1, :], full) for tile in live[g]]
            row[at] = jnp.where(inside, jnp.where(lane == base + k, 1.0, 0.0), row[at])
            rows.append(row)
        inv, lower = [], {}
        for j in range(8):
            inv.append(1.0 / small[j, j])
            for k in range(j + 1, 8):
                for m in range(k, 8):
                    small[k, m] = small[k, m] - (small[j, k] * small[j, m]) * inv[j]
            for k in range(j + 1, 8):
                lower[k, j] = small[j, k] * inv[j]
                rows[k] = [x - lower[k, j] * y for x, y in zip(rows[k], rows[j])]
        for j in range(8):
            pivot = small[j, j]
            root = lax.rsqrt(pivot)
            root = root * (1.5 - 0.5 * pivot * root * root)
            out = list(rows[j])
            for m in range(j, 8):
                out[at] = jnp.where(lane == base + m, small[j, m], out[at])
            for w in range(wide):
                rows_ref[8 * g + j:8 * g + j + 1, w * LANES:(w + 1) * LANES] = (out[w] * root)[:1, :]
        for work in fill[g::groups]:
            work()
        if g == groups - 1:
            break
        back = [[x * inv[k] for x in rows[k]] for k in range(8)]
        for k in range(7, -1, -1):
            for m in range(k):
                back[m] = [x - lower[k, m] * y for x, y in zip(back[m], back[k])]
        for i in range(g + 1, groups):
            total = None
            for k in range(8):
                col = jnp.broadcast_to(live[i][at][:, base + k:base + k + 1], full)
                term = [col * y for y in back[k]]
                total = term if total is None else [x + y for x, y in zip(total, term)]
            live[i] = [
                (jnp.where(inside, 0.0, x) if w == at else x) - y for w, (x, y) in enumerate(zip(live[i], total))
            ]


def panel(gram, offset, inv, lows):
    size = gram[0].shape[0]
    at, start = divmod(offset, LANES)
    lane = lax.broadcasted_iota(jnp.int32, (size, LANES), 1)
    inside = jnp.logical_and(lane >= start, lane < start + size)
    if offset == 0:
        return None, None, jnp.where(inside, gram[0], 0.0)
    value = jnp.concatenate(gram, axis=1) if at else gram[0]
    low = matmul(value, inv, (1, 1))
    lows[offset:offset + size, :(at + 1) * LANES] = low
    square = matmul(low, lows[at * LANES:(at + 1) * LANES, :(at + 1) * LANES], (1, 1))
    return low, matmul(low, inv), jnp.where(inside, gram[at] - square, 0.0)


def triangles(done, start):
    lane = lax.broadcasted_iota(jnp.int32, done.shape, 1)
    row = start + lax.broadcasted_iota(jnp.int32, done.shape, 0)
    upper = jnp.where(lane >= row, done, 0.0)
    return upper, jnp.where(lane < row, done, jnp.where(lane == row, 1.0 / done, 0.0))


def pieces(both, hi_ref, lo_ref, keep):
    deep, pixels = both.shape[1], hi_ref.shape[1]
    tall = both.shape[0] // 2

    def piece(at):
        cut = slice(at, at + 2 * LANES)
        value = product(both, hi_ref[:deep, cut], (1, 0)) + product(both, lo_ref[:deep, cut], (1, 0))
        keep(at, value[:tall] + value[tall:])

    return [functools.partial(piece, at) for at in range(0, pixels, 2 * LANES)]


def spread_rows(out32, tile_rows, tall, at, value):
    for i in range(2):
        out32[pl.ds(at // LANES + i, tall, stride=tile_rows), :] = value[:tall, i * LANES:(i + 1) * LANES]


def smooth_rows(read, rows):
    decay = math.exp(-1.0 / 6.0)
    tail = math.exp(-(REACH + 1) / 6.0)
    ahead = read(0)
    for p in range(1, REACH + 1):
        ahead = ahead * decay + read(p)
    out = [ahead]
    for i in range(1, rows):
        ahead = ahead * decay + (read(REACH + i) - tail * read(i - 1))
        out.append(ahead)
    last = REACH + rows - 1
    back = read(last + REACH) * decay
    for k in range(REACH - 1, 0, -1):
        back = (back + read(last + k)) * decay
    out[rows - 1] = out[rows - 1] + back
    for i in range(rows - 2, -1, -1):
        p = REACH + i
        back = (back + read(p + 1)) * decay - tail * read(p + REACH + 1)
        out[i] = out[i] + back
    return out


def shares(size, tiles, group):
    tall = size * (group * size // LANES + 1)
    return max(8, -(-tall // (8 * tiles)) * 8)


def exchange_kernel(ccds, tiles, pixel_total, frame_hbm, mask_hbm, good_hbm, w_hbm,
                    hi_ref, lo_ref, g_ref, x_ref, f_ref, early_ref,
                    good_ref, w_ref, frames, masks, flat, own, halo, done, lows, rows_ref, out32, *rest):
    bufs = [rest[4 * g:4 * g + 4] for g in range(GROUPS)]
    fs, ms, ws, hs, hr, s1, r1, s2, r2, s3, r3 = rest[4 * GROUPS:]
    exposures, tile_rows, h = frames.shape
    c, t = lax.axis_index("ccd"), lax.axis_index("tile")
    me, total = c * tiles + t, ccds * tiles
    after, before = lax.rem(me + 1, total), lax.rem(me + total - 1, total)
    after_id = (lax.div(after, tiles), lax.rem(after, tiles))
    before_id = (lax.div(before, tiles), lax.rem(before, tiles))
    part = exposures // CHUNKS
    size = exposures // GROUPS
    span = part * tile_rows
    scale = 1.0 / pixel_total
    loads = []
    small = [pltpu.make_async_copy(good_hbm, good_ref, ws.at[0]), pltpu.make_async_copy(w_hbm, w_ref, ws.at[1])]
    small[0].start()
    for k in range(CHUNKS):
        block = pl.ds(k * part, part)
        pair = (pltpu.make_async_copy(frame_hbm.at[block], frames.at[block], fs.at[k]),
                pltpu.make_async_copy(mask_hbm.at[block], masks.at[block], ms.at[k]))
        for copy in pair:
            copy.start()
        loads.append(pair)
    small[1].start()
    barrier = pltpu.get_barrier_semaphore()
    for peer in (before_id, after_id):
        pl.semaphore_signal(barrier, inc=1, device_id=peer, device_id_type=MESH)
    for d in range(1, tiles):
        pl.semaphore_signal(barrier, inc=1, device_id=(c, lax.rem(t + d, tiles)), device_id_type=MESH)
    for d in range(1, ccds):
        pl.semaphore_signal(barrier, inc=1, device_id=(lax.rem(c + d, ccds), t), device_id_type=MESH)
    small[0].wait()
    good = good_ref[...].astype(jnp.float32)[None]

    def mask(k):
        block = pl.ds(k * part, part)
        for copy in loads[k]:
            copy.wait()
        value = frames[block].astype(jnp.float32) * (masks[block].astype(jnp.float32) * good)
        flat[k % 2] = value.reshape(span, h)
        for r in range(tile_rows):
            own[k, r] = flat[k % 2, pl.ds(r, part, stride=tile_rows), :].astype(jnp.bfloat16)

    moves = []

    def send(k):
        pair = []
        for side, peer in enumerate((after_id, before_id)):
            copy = pltpu.make_async_remote_copy(
                src_ref=own.at[k], dst_ref=halo.at[side, k], send_sem=hs.at[side, k],
                recv_sem=hr.at[side, k], device_id=peer, device_id_type=MESH)
            copy.start()
            pair.append(copy)
        moves.append(pair)

    mask(0)
    pl.semaphore_wait(barrier, tiles + ccds)
    send(0)
    for k in range(1, CHUNKS):
        mask(k)
        if k < AHEAD:
            send(k)
    x_ref[...] = jnp.zeros(x_ref.shape, jnp.float32)
    f_ref[...] = jnp.zeros(f_ref.shape, jnp.float32)
    lows[...] = jnp.zeros(lows.shape, jnp.float32)
    for g in range(GROUPS):
        bufs[g][0][...] = jnp.zeros(bufs[g][0].shape, jnp.float32)
        if (g + 1) * size % LANES and g + 1 < GROUPS:
            for ref in (hi_ref, lo_ref):
                ref[(g + 1) * size:(g + 2) * size, :] = jnp.zeros((size, ref.shape[1]), jnp.bfloat16)
    has_before = jnp.where(me > 0, 1.0, 0.0)
    has_after = jnp.where(me < total - 1, 1.0, 0.0)
    small[1].wait()
    weights = w_ref[...]
    step = 16

    def smooth(k):
        @pl.loop(0, part // step)
        def _(n):
            some = pl.ds(pl.multiple_of(n * step, step), step)

            def read(p):
                if p < tile_rows:
                    return halo[0, k, p, some, :].astype(jnp.float32) * has_before
                if p < 2 * tile_rows:
                    return own[k, p - tile_rows, some, :].astype(jnp.float32)
                return halo[1, k, p - 2 * tile_rows, some, :].astype(jnp.float32) * has_after

            for r, value in enumerate(smooth_rows(read, tile_rows)):
                high, low = split(value)
                where = pl.ds(pl.multiple_of(r * part + n * step, step), step)
                done[where, :h] = high
                done[where, h:] = low

        value = product(done[...], weights, (1, 0))
        high, low = split(value[:, :h] + value[:, h:])
        rows = slice(k * part, (k + 1) * part)
        for r in range(tile_rows):
            hi_ref[rows, r * h:(r + 1) * h] = high[r * part:(r + 1) * part]
            lo_ref[rows, r * h:(r + 1) * h] = low[r * part:(r + 1) * part]

    sent = []
    waiting = {}

    def launch(g, stage):
        mine, near, far, whole = bufs[g]
        copies = []
        for d in range(1, ccds if stage == 2 else tiles):
            i = d - 1
            if stage == 1:
                peer = lax.rem(t + d, tiles)
                copy = pltpu.make_async_remote_copy(
                    src_ref=mine.at[peer], dst_ref=near.at[i], send_sem=s1.at[g, i], recv_sem=r1.at[g, i],
                    device_id=(c, peer), device_id_type=MESH)
            elif stage == 2:
                copy = pltpu.make_async_remote_copy(
                    src_ref=far.at[c], dst_ref=far.at[c], send_sem=s2.at[g, i], recv_sem=r2.at[g, i],
                    device_id=(lax.rem(c + d, ccds), t), device_id_type=MESH)
            else:
                copy = pltpu.make_async_remote_copy(
                    src_ref=whole.at[t], dst_ref=whole.at[t], send_sem=s3.at[g, i], recv_sem=r3.at[g, i],
                    device_id=(c, lax.rem(t + d, tiles)), device_id_type=MESH)
            copy.start()
            copies.append(copy)
        sent.extend(copies)
        waiting[g] = (stage, copies)

    def gram(g):
        first, stop = g * size, (g + 1) * size
        wide = (first // LANES + 1) * LANES
        some = jnp.concatenate([hi_ref[first:stop, :], lo_ref[first:stop, :]], axis=0)
        value = product(some, hi_ref[:wide, :], (1, 1)) + product(some, lo_ref[:wide, :], (1, 1))
        value = value[:size] + value[size:]
        packed = jnp.concatenate([value[:, w:w + LANES] for w in range(0, wide, LANES)], axis=0)
        mine = bufs[g][0]
        share = mine.shape[1]
        for i in range(packed.shape[0] // share):
            mine[i] = packed[i * share:(i + 1) * share]
        launch(g, 1)

    def advance(g):
        mine, near, far, whole = bufs[g]
        stage, copies = waiting[g]
        for copy in copies:
            copy.wait_recv()
        if stage == 1:
            value = mine[t]
            for d in range(1, tiles):
                value = value + near[d - 1]
            far[c] = value
            launch(g, 2)
        elif stage == 2:
            value = far[0]
            for i in range(1, ccds):
                value = value + far[i]
            whole[t] = value
            launch(g, 3)

    def factor(g):
        whole = bufs[g][3]
        value = whole[...].reshape(-1, LANES) * scale
        tiles_in = [value[w * size:(w + 1) * size] for w in range(g * size // LANES + 1)]
        rows = slice(g * size, (g + 1) * size)
        at, start = divmod(g * size, LANES)
        low, spread, block = panel(tiles_in, g * size, x_ref[:(at + 1) * LANES, :(at + 1) * LANES], lows)
        lane = lax.broadcasted_iota(jnp.int32, block.shape, 1)
        live = [block if low is None else jnp.where(lane < start, -spread[:, at * LANES:], block)]
        if at:
            live = [-spread[:, w * LANES:(w + 1) * LANES] for w in range(at)] + live
        fill = []
        if g:
            last = slice((g - 1) * size, g * size)
            deep = ((g - 1) * size // LANES + 1) * LANES
            both = jnp.concatenate(split(x_ref[last, :deep]), axis=0)
            fill = pieces(both, hi_ref, lo_ref, functools.partial(spread_rows, out32, tile_rows, size))
        eliminate(live, g * size, rows_ref, fill)
        cut = slice(at * LANES, (at + 1) * LANES)
        upper, lower = triangles(rows_ref[:, cut], start)
        x_ref[rows, cut] = lower
        f_ref[rows, cut] = upper if low is None else jnp.where(lane < start, low[:, cut], upper)
        if at:
            x_ref[rows, :at * LANES] = rows_ref[:, :at * LANES]
            f_ref[rows, :at * LANES] = low[:, :at * LANES]
        if g:
            early_ref[(g - 1) * size * tile_rows:g * size * tile_rows, :] = out32[...].astype(jnp.bfloat16)

    per = CHUNKS // GROUPS
    for k in range(CHUNKS):
        for copy in moves[k]:
            copy.wait_recv()
        if k % per == per - 1:
            for g in range(max(0, k // per - 3), k // per):
                advance(g)
        smooth(k)
        if k % per == per - 1:
            gram(k // per)
        if k + AHEAD < CHUNKS:
            send(k + AHEAD)
    for n in range(3):
        factor(GROUPS - 4 + n)
        for g in range(GROUPS - 1, GROUPS - 4 + n, -1):
            advance(g)
    g_ref[...] = bufs[GROUPS - 1][3][...]
    for copy in sum(moves, []) + sent:
        copy.wait_send()


def exchange(frames, source_mask, good_pixels, weights, pixel_total):
    ccds, tiles = lax.axis_size("ccd"), lax.axis_size("tile")
    exposures, tile_rows, _ = frames.shape
    pixels = tile_rows * LANES
    part, size = exposures // CHUNKS, exposures // GROUPS
    span = part * tile_rows
    dma = pltpu.SemaphoreType.DMA
    vm = pl.BlockSpec(memory_space=pltpu.VMEM)
    hbm = pl.BlockSpec(memory_space=pl.ANY)
    split_shape = pltpu.VMEM((exposures, pixels), jnp.bfloat16)
    square = pltpu.VMEM((exposures, exposures), jnp.float32)
    share = [shares(size, tiles, g) for g in range(GROUPS)]
    reduce = []
    for g in range(GROUPS):
        for n in (tiles, tiles - 1, ccds, tiles):
            reduce.append(pltpu.VMEM((n, share[g], LANES), jnp.float32))
    return pl.pallas_call(
        functools.partial(exchange_kernel, ccds, tiles, pixel_total),
        out_shape=(split_shape, split_shape, pltpu.VMEM((tiles, share[-1], LANES), jnp.float32), square, square,
                   pltpu.VMEM(((GROUPS - 2) * size * tile_rows, LANES), jnp.bfloat16)),
        in_specs=[hbm] * 4,
        out_specs=(vm,) * 6,
        scratch_shapes=[
            pltpu.VMEM(good_pixels.shape, jnp.int32),
            pltpu.VMEM(weights.shape, jnp.bfloat16),
            pltpu.VMEM(frames.shape, jnp.bfloat16),
            pltpu.VMEM(frames.shape, jnp.int32),
            pltpu.VMEM((2, span, LANES), jnp.float32),
            pltpu.VMEM((CHUNKS, tile_rows, part, LANES), jnp.bfloat16),
            pltpu.VMEM((2, CHUNKS, tile_rows, part, LANES), jnp.bfloat16),
            pltpu.VMEM((span, 2 * LANES), jnp.bfloat16),
            pltpu.VMEM((exposures, exposures), jnp.float32),
            pltpu.VMEM((size, exposures), jnp.float32),
            pltpu.VMEM((size * tile_rows, LANES), jnp.float32),
            *reduce,
            dma((CHUNKS,)), dma((CHUNKS,)), dma((2,)),
            dma((2, CHUNKS)), dma((2, CHUNKS)),
            dma((GROUPS, tiles - 1)), dma((GROUPS, tiles - 1)),
            dma((GROUPS, ccds - 1)), dma((GROUPS, ccds - 1)),
            dma((GROUPS, tiles - 1)), dma((GROUPS, tiles - 1)),
        ],
        compiler_params=pltpu.CompilerParams(collective_id=0, has_side_effects=True, vmem_limit_bytes=VMEM),
    )(*(pltpu.with_memory_space_constraint(x, pltpu.HBM) for x in (frames, source_mask, good_pixels, weights)))


def solve_kernel(pixel_total, g_ref, x_ref, f_ref, early_ref, hi_ref, lo_ref, o_hbm, b_hbm,
                 lows, rows_ref, out32, packed, rest_hi, rest_lo, factor, sems):
    exposures, pixels = hi_ref.shape
    tile_rows = pixels // LANES
    size = exposures // GROUPS
    span = size * tile_rows
    first = exposures - size
    at, start = divmod(first, LANES)
    copies = []

    def out(src, dst):
        copy = pltpu.make_async_copy(src, dst, sems.at[len(copies)])
        copy.start()
        copies.append(copy)

    out(early_ref, b_hbm.at[pl.ds(0, early_ref.shape[0])])
    lows[...] = jnp.zeros(lows.shape, jnp.float32)
    value = g_ref[...].reshape(-1, LANES) * (1.0 / pixel_total)
    low, spread, block = panel([value[w * size:(w + 1) * size] for w in range(at + 1)], first, x_ref[...], lows)
    row = first + lax.broadcasted_iota(jnp.int32, (size, exposures), 0)
    col = lax.broadcasted_iota(jnp.int32, (size, exposures), 1)
    rest = jnp.where(col < first, -spread, jnp.where(col == row, 1.0, 0.0))
    xh, xl = split(x_ref[first - size:first, :])
    rh, rl = split(rest)
    both = jnp.concatenate([xh, rh, xl, rl], axis=0)

    def keep(cut, value):
        spread_rows(out32, tile_rows, size, cut, value)
        high, small = split(value[size:])
        rest_hi[:, cut:cut + 2 * LANES] = high
        rest_lo[:, cut:cut + 2 * LANES] = small

    eliminate([block], start, rows_ref, pieces(both, hi_ref, lo_ref, keep))
    upper, lower = triangles(rows_ref[...], start)
    packed[:span, :] = out32[...].astype(jnp.bfloat16)
    out(packed.at[pl.ds(0, span)], b_hbm.at[pl.ds((exposures - 2 * size) * tile_rows, span)])
    both = jnp.concatenate(split(lower[:, start:start + size]), axis=0)
    for piece in pieces(both, rest_hi, rest_lo, functools.partial(spread_rows, out32, tile_rows, size)):
        piece()
    packed[span:, :] = out32[...].astype(jnp.bfloat16)
    out(packed.at[pl.ds(span, span)], b_hbm.at[pl.ds(first * tile_rows, span)])
    whole = jnp.where(col < first, low, jnp.pad(upper, ((0, 0), (at * LANES, 0))) if at else upper)
    whole = jnp.concatenate([f_ref[:first, :], whole], axis=0)
    row = lax.broadcasted_iota(jnp.int32, (exposures, exposures), 0) // size
    col = lax.broadcasted_iota(jnp.int32, (exposures, exposures), 1) // size
    factor[...] = jnp.where(row == col, whole, 0.0) + jnp.where(col < row, whole, 0.0).T
    out(factor, o_hbm)
    for copy in copies:
        copy.wait()


def solve(gram, x, f, early, hi, lo, pixel_total):
    exposures, pixels = hi.shape
    size = exposures // GROUPS
    span = size * pixels // LANES
    vm = pl.BlockSpec(memory_space=pltpu.VMEM)
    hbm = pl.BlockSpec(memory_space=pl.ANY)
    square = (exposures, exposures)
    rows = (exposures * pixels // LANES, LANES)
    given = (pltpu.with_memory_space_constraint(value, pltpu.VMEM) for value in (gram, x, f, early, hi, lo))
    return pl.pallas_call(
        functools.partial(solve_kernel, pixel_total),
        out_shape=(jax.ShapeDtypeStruct(square, jnp.float32), jax.ShapeDtypeStruct(rows, jnp.bfloat16)),
        in_specs=[vm] * 6,
        out_specs=(hbm, hbm),
        scratch_shapes=[
            pltpu.VMEM(square, jnp.float32),
            pltpu.VMEM((size, LANES), jnp.float32),
            pltpu.VMEM((span, LANES), jnp.float32),
            pltpu.VMEM((2 * span, LANES), jnp.bfloat16),
            pltpu.VMEM((size, pixels), jnp.bfloat16),
            pltpu.VMEM((size, pixels), jnp.bfloat16),
            pltpu.VMEM(square, jnp.float32),
            pltpu.SemaphoreType.DMA((4,)),
        ],
        compiler_params=pltpu.CompilerParams(vmem_limit_bytes=VMEM),
    )(*given)


def per_device(frames, source_mask, good_pixels):
    exposures, tile_rows, tile_cols = frames.shape
    tiles = lax.axis_size("tile")
    pixel_total = float(tile_rows * tile_cols * lax.axis_size("ccd") * tiles)
    hi, lo, gram, x, f, early = exchange(frames, source_mask, good_pixels, column_matrix(tile_cols), pixel_total)
    factor, basis = solve(gram, x, f, early, hi, lo, pixel_total)
    return (factor, basis.reshape(exposures, tile_rows, tile_cols))


def solution(mesh):
    in_specs = (
        P(None, ("ccd", "tile"), None),
        P(None, ("ccd", "tile"), None),
        P(("ccd", "tile"), None),
    )
    out_specs = (P(), P(None, ("ccd", "tile"), None))
    return jax.shard_map(
        per_device, mesh=mesh, in_specs=in_specs, out_specs=out_specs, check_vma=False
    )
```

```python
import functools
import math

import jax
import jax.numpy as jnp
import numpy as np
from jax import lax
from jax.experimental import pallas as pl
from jax.experimental.pallas import tpu as pltpu
from jax.sharding import PartitionSpec as P

REACH = 16
MESH = pl.DeviceIdType.MESH
HIGH = lax.Precision.HIGHEST
LANES = 128
CHUNKS = 16
BOUNDS = (0, 4, 8, 12, 14, 16)
GROUPS = len(BOUNDS) - 1
AHEAD = 4
SLOTS = {8: (0,), 12: (1,), 13: (0,), 15: (2,)}
FIRST = 13
TAIL = (((3, 1), 1), ((4, 2), 2), ((3,), 3), ((4,), None))
VMEM = 40 << 20


def column_matrix(tile_cols):
    distance = np.abs(np.arange(tile_cols)[:, None] - np.arange(tile_cols)[None, :])
    norm = np.sum(np.exp(-2.0 * np.abs(np.arange(-REACH, REACH + 1)) / 6.0))
    full = np.where(distance <= REACH, np.exp(-distance / 6.0) / norm, 0.0).astype(np.float32)
    high = full.astype(jnp.bfloat16)
    low = (full - high.astype(np.float32)).astype(jnp.bfloat16)
    pair = np.concatenate([high, low], axis=1)
    return np.concatenate([pair, pair], axis=0)


def matmul(a, b, contract=(1, 0)):
    return lax.dot_general(
        a, b, (((contract[0],), (contract[1],)), ((), ())), precision=HIGH, preferred_element_type=jnp.float32
    )


def split(value):
    high = value.astype(jnp.bfloat16)
    return high, (value - high.astype(jnp.float32)).astype(jnp.bfloat16)


def product(a, b, contract):
    return lax.dot_general(
        a, b, (((contract[0],), (contract[1],)), ((), ())), preferred_element_type=jnp.float32
    )


def eliminate(block, offset, rows_ref, fill=()):
    size = block[0].shape[0]
    groups, wide = size // 8, len(block)
    at, start = divmod(offset, LANES)
    full = (8, LANES)
    live = [[tile[8 * g:8 * g + 8, :] for tile in block] for g in range(groups)]
    lane = lax.broadcasted_iota(jnp.int32, full, 1)
    for g in range(groups):
        base = start + 8 * g
        inside = jnp.logical_and(lane >= base, lane < base + 8)
        cols = [jnp.broadcast_to(live[g][at][:, base + k:base + k + 1], full) for k in range(8)]
        small = {(j, k): jnp.broadcast_to(cols[k][j:j + 1, :], full) for j in range(8) for k in range(j, 8)}
        rows = []
        for k in range(8):
            row = [jnp.broadcast_to(tile[k:k + 1, :], full) for tile in live[g]]
            row[at] = jnp.where(inside, jnp.where(lane == base + k, 1.0, 0.0), row[at])
            rows.append(row)
        inv, lower = [], {}
        for j in range(8):
            inv.append(1.0 / small[j, j])
            for k in range(j + 1, 8):
                for m in range(k, 8):
                    small[k, m] = small[k, m] - (small[j, k] * small[j, m]) * inv[j]
            for k in range(j + 1, 8):
                lower[k, j] = small[j, k] * inv[j]
                rows[k] = [x - lower[k, j] * y for x, y in zip(rows[k], rows[j])]
        for j in range(8):
            pivot = small[j, j]
            root = lax.rsqrt(pivot)
            root = root * (1.5 - 0.5 * pivot * root * root)
            out = list(rows[j])
            for m in range(j, 8):
                out[at] = jnp.where(lane == base + m, small[j, m], out[at])
            for w in range(wide):
                rows_ref[8 * g + j:8 * g + j + 1, w * LANES:(w + 1) * LANES] = (out[w] * root)[:1, :]
        for work in fill[g::groups]:
            work()
        if g == groups - 1:
            break
        back = [[x * inv[k] for x in rows[k]] for k in range(8)]
        for k in range(7, -1, -1):
            for m in range(k):
                back[m] = [x - lower[k, m] * y for x, y in zip(back[m], back[k])]
        for i in range(g + 1, groups):
            total = None
            for k in range(8):
                col = jnp.broadcast_to(live[i][at][:, base + k:base + k + 1], full)
                term = [col * y for y in back[k]]
                total = term if total is None else [x + y for x, y in zip(total, term)]
            live[i] = [
                (jnp.where(inside, 0.0, x) if w == at else x) - y for w, (x, y) in enumerate(zip(live[i], total))
            ]


def panel(gram, offset, inv, lows):
    size = gram[0].shape[0]
    at, start = divmod(offset, LANES)
    lane = lax.broadcasted_iota(jnp.int32, (size, LANES), 1)
    inside = jnp.logical_and(lane >= start, lane < start + size)
    if offset == 0:
        return None, None, jnp.where(inside, gram[0], 0.0)
    value = jnp.concatenate(gram, axis=1) if at else gram[0]
    low = matmul(value, inv, (1, 1))
    lows[offset:offset + size, :(at + 1) * LANES] = low
    square = matmul(low, lows[at * LANES:(at + 1) * LANES, :(at + 1) * LANES], (1, 1))
    return low, matmul(low, inv), jnp.where(inside, gram[at] - square, 0.0)


def triangles(done, start):
    lane = lax.broadcasted_iota(jnp.int32, done.shape, 1)
    row = start + lax.broadcasted_iota(jnp.int32, done.shape, 0)
    upper = jnp.where(lane >= row, done, 0.0)
    return upper, jnp.where(lane < row, done, jnp.where(lane == row, 1.0 / done, 0.0))


def pieces(both, hi_ref, lo_ref, keep):
    deep, pixels = both.shape[1], hi_ref.shape[1]
    tall = both.shape[0] // 2

    def piece(at):
        cut = slice(at, at + 2 * LANES)
        value = product(both, hi_ref[:deep, cut], (1, 0)) + product(both, lo_ref[:deep, cut], (1, 0))
        keep(at, value[:tall] + value[tall:])

    return [functools.partial(piece, at) for at in range(0, pixels, 2 * LANES)]


def spread_rows(out32, tile_rows, tall, at, value):
    for i in range(2):
        out32[pl.ds(at // LANES + i, tall, stride=tile_rows), :] = value[:tall, i * LANES:(i + 1) * LANES]


def smooth_rows(read, rows):
    decay = math.exp(-1.0 / 6.0)
    tail = math.exp(-(REACH + 1) / 6.0)
    ahead = read(0)
    for p in range(1, REACH + 1):
        ahead = ahead * decay + read(p)
    out = [ahead]
    for i in range(1, rows):
        ahead = ahead * decay + (read(REACH + i) - tail * read(i - 1))
        out.append(ahead)
    last = REACH + rows - 1
    back = read(last + REACH) * decay
    for k in range(REACH - 1, 0, -1):
        back = (back + read(last + k)) * decay
    out[rows - 1] = out[rows - 1] + back
    for i in range(rows - 2, -1, -1):
        p = REACH + i
        back = (back + read(p + 1)) * decay - tail * read(p + REACH + 1)
        out[i] = out[i] + back
    return out


def group_rows(exposures, group):
    part = exposures // CHUNKS
    return BOUNDS[group] * part, BOUNDS[group + 1] * part


def shares(exposures, total, group):
    first, stop = group_rows(exposures, group)
    tall = (stop - first) * (first // LANES + 1)
    return tall, -(-tall // total)


def exchange_kernel(ccds, tiles, pixel_total, frame_hbm, mask_hbm, good_hbm, w_hbm,
                    hi_ref, lo_ref, g_ref, x_ref, f_ref, early_ref,
                    good_ref, w_ref, frames, masks, flat, own, halo, done, lows, rows_ref, out32, *rest):
    bufs = [rest[3 * g:3 * g + 3] for g in range(GROUPS)]
    fs, ms, ws, hs, hr, s1, r1, s2, r2, ready = rest[3 * GROUPS:]
    exposures, tile_rows, h = frames.shape
    c, t = lax.axis_index("ccd"), lax.axis_index("tile")
    me, total = c * tiles + t, ccds * tiles
    after, before = lax.rem(me + 1, total), lax.rem(me + total - 1, total)
    after_id = (lax.div(after, tiles), lax.rem(after, tiles))
    before_id = (lax.div(before, tiles), lax.rem(before, tiles))
    part = exposures // CHUNKS
    span = part * tile_rows
    scale = 1.0 / pixel_total
    loads = []
    small = [pltpu.make_async_copy(good_hbm, good_ref, ws.at[0]), pltpu.make_async_copy(w_hbm, w_ref, ws.at[1])]
    small[0].start()
    for k in range(CHUNKS):
        block = pl.ds(k * part, part)
        pair = (pltpu.make_async_copy(frame_hbm.at[block], frames.at[block], fs.at[k]),
                pltpu.make_async_copy(mask_hbm.at[block], masks.at[block], ms.at[k]))
        for copy in pair:
            copy.start()
        loads.append(pair)
    small[1].start()
    barrier = pltpu.get_barrier_semaphore()
    for peer in (before_id, after_id):
        pl.semaphore_signal(barrier, inc=1, device_id=peer, device_id_type=MESH)
    for d in range(1, tiles):
        pl.semaphore_signal(barrier, inc=1, device_id=(c, lax.rem(t + d, tiles)), device_id_type=MESH)
    for d in range(1, ccds):
        pl.semaphore_signal(barrier, inc=1, device_id=(lax.rem(c + d, ccds), t), device_id_type=MESH)
    small[0].wait()
    good = good_ref[...].astype(jnp.float32)[None]

    def mask(k):
        block = pl.ds(k * part, part)
        for copy in loads[k]:
            copy.wait()
        value = frames[block].astype(jnp.float32) * (masks[block].astype(jnp.float32) * good)
        flat[k % 2] = value.reshape(span, h)
        for r in range(tile_rows):
            own[k, r] = flat[k % 2, pl.ds(r, part, stride=tile_rows), :].astype(jnp.bfloat16)

    moves = []

    def send(k):
        pair = []
        for side, peer in enumerate((after_id, before_id)):
            copy = pltpu.make_async_remote_copy(
                src_ref=own.at[k], dst_ref=halo.at[side, k], send_sem=hs.at[side, k],
                recv_sem=hr.at[side, k], device_id=peer, device_id_type=MESH)
            copy.start()
            pair.append(copy)
        moves.append(pair)

    mask(0)
    pl.semaphore_wait(barrier, tiles + ccds)
    send(0)
    for d in range(1, ccds):
        pl.semaphore_signal(ready, inc=1, device_id=(lax.rem(c + d, ccds), t), device_id_type=MESH)
    for k in range(1, CHUNKS):
        mask(k)
        if k < AHEAD:
            send(k)
    x_ref[...] = jnp.zeros(x_ref.shape, jnp.float32)
    f_ref[...] = jnp.zeros(f_ref.shape, jnp.float32)
    lows[...] = jnp.zeros(lows.shape, jnp.float32)
    for g in range(GROUPS):
        bufs[g][0][...] = jnp.zeros(bufs[g][0].shape, jnp.float32)
        first, stop = group_rows(exposures, g)
        left = LANES - stop % LANES
        if first % LANES == 0 and left < LANES:
            for ref in (hi_ref, lo_ref):
                ref[stop:stop + left, :] = jnp.zeros((left, ref.shape[1]), jnp.bfloat16)
    has_before = jnp.where(me > 0, 1.0, 0.0)
    has_after = jnp.where(me < total - 1, 1.0, 0.0)
    small[1].wait()
    weights = w_ref[...]
    step = 16

    def smooth(k):
        @pl.loop(0, part // step)
        def _(n):
            some = pl.ds(pl.multiple_of(n * step, step), step)

            def read(p):
                if p < tile_rows:
                    return halo[0, k, p, some, :].astype(jnp.float32) * has_before
                if p < 2 * tile_rows:
                    return own[k, p - tile_rows, some, :].astype(jnp.float32)
                return halo[1, k, p - 2 * tile_rows, some, :].astype(jnp.float32) * has_after

            for r, value in enumerate(smooth_rows(read, tile_rows)):
                high, low = split(value)
                where = pl.ds(pl.multiple_of(r * part + n * step, step), step)
                done[where, :h] = high
                done[where, h:] = low

        value = product(done[...], weights, (1, 0))
        high, low = split(value[:, :h] + value[:, h:])
        rows = slice(k * part, (k + 1) * part)
        for r in range(tile_rows):
            hi_ref[rows, r * h:(r + 1) * h] = high[r * part:(r + 1) * part]
            lo_ref[rows, r * h:(r + 1) * h] = low[r * part:(r + 1) * part]

    stages = {}

    def every(body):
        if total <= 64:
            for d in sorted(range(1, total), key=lambda d: -min(d, total - d)):
                body(d)
        else:
            pl.loop(1, total)(body)

    def move(g, stage, src, dst, peer):
        send_sem, recv_sem = ((s1, r1), (s2, r2))[stage]
        return pltpu.make_async_remote_copy(
            src_ref=src, dst_ref=dst, send_sem=send_sem.at[g], recv_sem=recv_sem.at[g],
            device_id=(lax.div(peer, tiles), lax.rem(peer, tiles)), device_id_type=MESH)

    def all_of(g, stage):
        ref = bufs[g][1 + stage].at[pl.ds(0, total - 1)]
        return move(g, stage, ref, ref, after)

    def launch(g, stage):
        mine, near, whole = bufs[g]

        def body(d):
            peer = lax.rem(me + d, total)
            if stage == 0:
                move(g, 0, mine.at[peer], near.at[d - 1], peer).start()
            else:
                move(g, 1, whole.at[me], whole.at[me], peer).start()

        every(body)
        stages[g] = stage

    def gram(g):
        first, stop = group_rows(exposures, g)
        size = stop - first
        wide = (first // LANES + 1) * LANES
        some = jnp.concatenate([hi_ref[first:stop, :], lo_ref[first:stop, :]], axis=0)
        value = product(some, hi_ref[:wide, :], (1, 1)) + product(some, lo_ref[:wide, :], (1, 1))
        value = value[:size] + value[size:]
        packed = jnp.concatenate([value[:, w:w + LANES] for w in range(0, wide, LANES)], axis=0)
        mine = bufs[g][0]
        share = mine.shape[1]
        if g == 0:
            pl.semaphore_wait(ready, ccds - 1)
        for i in range(packed.shape[0] // share):
            mine[i] = packed[i * share:(i + 1) * share]
        launch(g, 0)

    def advance(g):
        mine, near, whole = bufs[g]
        all_of(g, stages[g]).wait_recv()
        if stages[g] == 0:
            whole[me] = mine[me] + jnp.sum(near[:total - 1], axis=0)
            launch(g, 1)

    def gathered(g, ref):
        whole = bufs[g][2]
        tall, share = shares(exposures, total, g)
        for i in range(tall // share):
            ref[i * share:(i + 1) * share, :] = whole[i]
        return tall

    def factor(g):
        value = flat[0, :gathered(g, flat.at[0]), :] * scale
        first, stop = group_rows(exposures, g)
        size, rows = stop - first, slice(first, stop)
        at, start = divmod(first, LANES)
        tiles_in = [value[w * size:(w + 1) * size] for w in range(at + 1)]
        low, spread, block = panel(tiles_in, first, x_ref[:(at + 1) * LANES, :(at + 1) * LANES], lows)
        lane = lax.broadcasted_iota(jnp.int32, block.shape, 1)
        live = [block if low is None else jnp.where(lane < start, -spread[:, at * LANES:], block)]
        if at:
            live = [-spread[:, w * LANES:(w + 1) * LANES] for w in range(at)] + live
        fill = []
        if g:
            last = group_rows(exposures, g - 1)
            deep = (last[0] // LANES + 1) * LANES
            both = jnp.concatenate(split(x_ref[last[0]:last[1], :deep]), axis=0)
            fill = pieces(both, hi_ref, lo_ref, functools.partial(spread_rows, out32, tile_rows, last[1] - last[0]))
        eliminate(live, first, rows_ref, fill)
        cut = slice(at * LANES, (at + 1) * LANES)
        upper, lower = triangles(rows_ref[:size, cut], start)
        x_ref[rows, cut] = lower
        f_ref[rows, cut] = upper if low is None else jnp.where(lane < start, low[:, cut], upper)
        if at:
            x_ref[rows, :at * LANES] = rows_ref[:size, :at * LANES]
            f_ref[rows, :at * LANES] = low[:, :at * LANES]
        if g:
            tall = (last[1] - last[0]) * tile_rows
            early_ref[last[0] * tile_rows:last[1] * tile_rows, :] = out32[:tall, :].astype(jnp.bfloat16)

    for k in range(CHUNKS):
        for copy in moves[k]:
            copy.wait_recv()
        for g in SLOTS.get(k, ()):
            advance(g)
        smooth(k)
        if k + 1 in BOUNDS:
            gram(BOUNDS.index(k + 1) - 1)
        if k + AHEAD < CHUNKS:
            send(k + AHEAD)
        if k == FIRST:
            factor(0)
    for order, g in TAIL:
        for i in order:
            advance(i)
        if g is not None:
            factor(g)
    gathered(GROUPS - 1, g_ref)
    for g in range(GROUPS):
        for stage in range(2):
            all_of(g, stage).wait_send()
    for copy in sum(moves, []):
        copy.wait_send()


def exchange(frames, source_mask, good_pixels, weights, pixel_total):
    ccds, tiles = lax.axis_size("ccd"), lax.axis_size("tile")
    exposures, tile_rows, _ = frames.shape
    pixels = tile_rows * LANES
    part = exposures // CHUNKS
    span = part * tile_rows
    size = max(stop - first for first, stop in (group_rows(exposures, g) for g in range(GROUPS)))
    early = group_rows(exposures, GROUPS - 2)[0]
    dma = pltpu.SemaphoreType.DMA
    vm = pl.BlockSpec(memory_space=pltpu.VMEM)
    hbm = pl.BlockSpec(memory_space=pl.ANY)
    split_shape = pltpu.VMEM((exposures, pixels), jnp.bfloat16)
    square = pltpu.VMEM((exposures, exposures), jnp.float32)
    share = [shares(exposures, ccds * tiles, g) for g in range(GROUPS)]
    reduce = []
    for g in range(GROUPS):
        reduce += [pltpu.VMEM((ccds * tiles, share[g][1], LANES), jnp.float32)] * 3
    return pl.pallas_call(
        functools.partial(exchange_kernel, ccds, tiles, pixel_total),
        out_shape=(split_shape, split_shape, pltpu.VMEM((share[-1][0], LANES), jnp.float32), square, square,
                   pltpu.VMEM((early * tile_rows, LANES), jnp.bfloat16)),
        in_specs=[hbm] * 4,
        out_specs=(vm,) * 6,
        scratch_shapes=[
            pltpu.VMEM(good_pixels.shape, jnp.int32),
            pltpu.VMEM(weights.shape, jnp.bfloat16),
            pltpu.VMEM(frames.shape, jnp.bfloat16),
            pltpu.VMEM(frames.shape, jnp.int32),
            pltpu.VMEM((2, span, LANES), jnp.float32),
            pltpu.VMEM((CHUNKS, tile_rows, part, LANES), jnp.bfloat16),
            pltpu.VMEM((2, CHUNKS, tile_rows, part, LANES), jnp.bfloat16),
            pltpu.VMEM((span, 2 * LANES), jnp.bfloat16),
            pltpu.VMEM((exposures, exposures), jnp.float32),
            pltpu.VMEM((size, exposures), jnp.float32),
            pltpu.VMEM((size * tile_rows, LANES), jnp.float32),
            *reduce,
            dma((CHUNKS,)), dma((CHUNKS,)), dma((2,)),
            dma((2, CHUNKS)), dma((2, CHUNKS)),
            dma((GROUPS,)), dma((GROUPS,)), dma((GROUPS,)), dma((GROUPS,)),
            pltpu.SemaphoreType.REGULAR,
        ],
        compiler_params=pltpu.CompilerParams(collective_id=0, has_side_effects=True, vmem_limit_bytes=VMEM),
    )(*(pltpu.with_memory_space_constraint(x, pltpu.HBM) for x in (frames, source_mask, good_pixels, weights)))


def solve_kernel(pixel_total, g_ref, x_ref, f_ref, early_ref, hi_ref, lo_ref, o_hbm, b_hbm,
                 lows, rows_ref, out32, packed, rest_hi, rest_lo, factor, sems):
    exposures, pixels = hi_ref.shape
    tile_rows = pixels // LANES
    before, first = group_rows(exposures, GROUPS - 2)
    size, prior = exposures - first, first - before
    at, start = divmod(first, LANES)
    copies = []

    def out(src, dst):
        copy = pltpu.make_async_copy(src, dst, sems.at[len(copies)])
        copy.start()
        copies.append(copy)

    out(early_ref, b_hbm.at[pl.ds(0, early_ref.shape[0])])
    lows[...] = jnp.zeros(lows.shape, jnp.float32)
    value = g_ref[...] * (1.0 / pixel_total)
    low, spread, block = panel([value[w * size:(w + 1) * size] for w in range(at + 1)], first, x_ref[...], lows)
    row = first + lax.broadcasted_iota(jnp.int32, (size, exposures), 0)
    col = lax.broadcasted_iota(jnp.int32, (size, exposures), 1)
    rest = jnp.where(col < first, -spread, jnp.where(col == row, 1.0, 0.0))
    xh, xl = split(x_ref[before:first, :])
    rh, rl = split(rest)
    both = jnp.concatenate([xh, rh, xl, rl], axis=0)

    def keep(cut, value):
        spread_rows(out32, tile_rows, prior, cut, value)
        high, small = split(value[prior:])
        rest_hi[:, cut:cut + 2 * LANES] = high
        rest_lo[:, cut:cut + 2 * LANES] = small

    def rows_out(top, stop):
        tall = (stop - top) * tile_rows
        here = pl.ds((top - before) * tile_rows, tall)
        packed[here, :] = out32[:tall, :].astype(jnp.bfloat16)
        out(packed.at[here], b_hbm.at[pl.ds(top * tile_rows, tall)])

    def upper_rows():
        whole = jnp.concatenate([f_ref[:first, :], jnp.where(col < first, low, 0.0)], axis=0)
        down = lax.broadcasted_iota(jnp.int32, (exposures, exposures), 0)
        over = lax.broadcasted_iota(jnp.int32, (exposures, exposures), 1)
        same = over < 0
        for g in range(GROUPS - 1):
            a, b = group_rows(exposures, g)
            ranges = [jnp.logical_and(i >= a, i < b) for i in (down, over)]
            same = jnp.logical_or(same, jnp.logical_and(*ranges))
        both_sides = jnp.where(same, whole, 0.0) + jnp.where(jnp.logical_or(same, over > down), 0.0, whole).T
        factor[:first, :] = both_sides[:first]
        out(factor.at[pl.ds(0, first)], o_hbm.at[pl.ds(0, first)])

    fill = [upper_rows] + pieces(both, hi_ref, lo_ref, keep)
    eliminate([block], start, rows_ref, fill)
    upper, lower = triangles(rows_ref[...], start)
    rows_out(before, first)
    if at:
        factor[first:, :at * LANES] = jnp.zeros((size, at * LANES), jnp.float32)
    factor[first:, at * LANES:] = upper
    out(factor.at[pl.ds(first, size)], o_hbm.at[pl.ds(first, size)])
    both = jnp.concatenate(split(lower[:, start:start + size]), axis=0)
    for piece in pieces(both, rest_hi, rest_lo, functools.partial(spread_rows, out32, tile_rows, size)):
        piece()
    rows_out(first, exposures)
    for copy in copies:
        copy.wait()


def solve(gram, x, f, early, hi, lo, pixel_total):
    exposures, pixels = hi.shape
    before, first = group_rows(exposures, GROUPS - 2)
    size, tile_rows = exposures - first, pixels // LANES
    vm = pl.BlockSpec(memory_space=pltpu.VMEM)
    hbm = pl.BlockSpec(memory_space=pl.ANY)
    square = (exposures, exposures)
    rows = (exposures * pixels // LANES, LANES)
    given = (pltpu.with_memory_space_constraint(value, pltpu.VMEM) for value in (gram, x, f, early, hi, lo))
    return pl.pallas_call(
        functools.partial(solve_kernel, pixel_total),
        out_shape=(jax.ShapeDtypeStruct(square, jnp.float32), jax.ShapeDtypeStruct(rows, jnp.bfloat16)),
        in_specs=[vm] * 6,
        out_specs=(hbm, hbm),
        scratch_shapes=[
            pltpu.VMEM(square, jnp.float32),
            pltpu.VMEM((size, LANES), jnp.float32),
            pltpu.VMEM((max(size, first - before) * tile_rows, LANES), jnp.float32),
            pltpu.VMEM(((exposures - before) * tile_rows, LANES), jnp.bfloat16),
            pltpu.VMEM((size, pixels), jnp.bfloat16),
            pltpu.VMEM((size, pixels), jnp.bfloat16),
            pltpu.VMEM(square, jnp.float32),
            pltpu.SemaphoreType.DMA((5,)),
        ],
        compiler_params=pltpu.CompilerParams(vmem_limit_bytes=VMEM),
    )(*given)


def per_device(frames, source_mask, good_pixels):
    exposures, tile_rows, tile_cols = frames.shape
    tiles = lax.axis_size("tile")
    pixel_total = float(tile_rows * tile_cols * lax.axis_size("ccd") * tiles)
    hi, lo, gram, x, f, early = exchange(frames, source_mask, good_pixels, column_matrix(tile_cols), pixel_total)
    factor, basis = solve(gram, x, f, early, hi, lo, pixel_total)
    return (factor, basis.reshape(exposures, tile_rows, tile_cols))


def solution(mesh):
    in_specs = (
        P(None, ("ccd", "tile"), None),
        P(None, ("ccd", "tile"), None),
        P(("ccd", "tile"), None),
    )
    out_specs = (P(), P(None, ("ccd", "tile"), None))
    return jax.shard_map(
        per_device, mesh=mesh, in_specs=in_specs, out_specs=out_specs, check_vma=False
    )
```

```python
import functools
import math

import jax
import jax.numpy as jnp
import numpy as np
from jax import lax
from jax.experimental import pallas as pl
from jax.experimental.pallas import tpu as pltpu
from jax.sharding import PartitionSpec as P

REACH = 16
MESH = pl.DeviceIdType.MESH
HIGH = lax.Precision.HIGHEST
LANES = 128
CHUNKS = 16
BOUNDS = (0, 4, 8, 12, 14, 16)
GROUPS = len(BOUNDS) - 1
AHEAD = 4
SLOTS = {8: (0,), 12: (1,), 13: (0,), 15: (2,)}
FIRST = 13
BESIDE = {1: 0, 3: 2}
BEHIND = (1,)
TAIL = (((3, 1), 1), ((4, 2), 2), ((3,), 3), ((4,), None))
VMEM = 40 << 20


def column_matrix(tile_cols):
    distance = np.abs(np.arange(tile_cols)[:, None] - np.arange(tile_cols)[None, :])
    norm = np.sum(np.exp(-2.0 * np.abs(np.arange(-REACH, REACH + 1)) / 6.0))
    full = np.where(distance <= REACH, np.exp(-distance / 6.0) / norm, 0.0).astype(np.float32)
    high = full.astype(jnp.bfloat16)
    low = (full - high.astype(np.float32)).astype(jnp.bfloat16)
    pair = np.concatenate([high, low], axis=1)
    return np.concatenate([pair, pair], axis=0)


def matmul(a, b, contract=(1, 0)):
    return lax.dot_general(
        a, b, (((contract[0],), (contract[1],)), ((), ())), precision=HIGH, preferred_element_type=jnp.float32
    )


def split(value):
    high = value.astype(jnp.bfloat16)
    return high, (value - high.astype(jnp.float32)).astype(jnp.bfloat16)


def product(a, b, contract):
    return lax.dot_general(
        a, b, (((contract[0],), (contract[1],)), ((), ())), preferred_element_type=jnp.float32
    )


def eliminate(block, offset, rows_ref, fill=()):
    size = block[0].shape[0]
    groups, wide = size // 8, len(block)
    at, start = divmod(offset, LANES)
    full = (8, LANES)
    live = [[tile[8 * g:8 * g + 8, :] for tile in block] for g in range(groups)]
    lane = lax.broadcasted_iota(jnp.int32, full, 1)
    for g in range(groups):
        base = start + 8 * g
        inside = jnp.logical_and(lane >= base, lane < base + 8)
        cols = [jnp.broadcast_to(live[g][at][:, base + k:base + k + 1], full) for k in range(8)]
        small = {(j, k): jnp.broadcast_to(cols[k][j:j + 1, :], full) for j in range(8) for k in range(j, 8)}
        rows = []
        for k in range(8):
            row = [jnp.broadcast_to(tile[k:k + 1, :], full) for tile in live[g]]
            row[at] = jnp.where(inside, jnp.where(lane == base + k, 1.0, 0.0), row[at])
            rows.append(row)
        inv, lower = [], {}
        for j in range(8):
            inv.append(1.0 / small[j, j])
            for k in range(j + 1, 8):
                for m in range(k, 8):
                    small[k, m] = small[k, m] - (small[j, k] * small[j, m]) * inv[j]
            for k in range(j + 1, 8):
                lower[k, j] = small[j, k] * inv[j]
                rows[k] = [x - lower[k, j] * y for x, y in zip(rows[k], rows[j])]
        for j in range(8):
            pivot = small[j, j]
            root = lax.rsqrt(pivot)
            root = root * (1.5 - 0.5 * pivot * root * root)
            out = list(rows[j])
            for m in range(j, 8):
                out[at] = jnp.where(lane == base + m, small[j, m], out[at])
            for w in range(wide):
                rows_ref[8 * g + j:8 * g + j + 1, w * LANES:(w + 1) * LANES] = (out[w] * root)[:1, :]
        for work in fill[g::groups]:
            work()
        if g == groups - 1:
            break
        back = [[x * inv[k] for x in rows[k]] for k in range(8)]
        for k in range(7, -1, -1):
            for m in range(k):
                back[m] = [x - lower[k, m] * y for x, y in zip(back[m], back[k])]
        for i in range(g + 1, groups):
            total = None
            for k in range(8):
                col = jnp.broadcast_to(live[i][at][:, base + k:base + k + 1], full)
                term = [col * y for y in back[k]]
                total = term if total is None else [x + y for x, y in zip(total, term)]
            live[i] = [
                (jnp.where(inside, 0.0, x) if w == at else x) - y for w, (x, y) in enumerate(zip(live[i], total))
            ]


def panel(gram, offset, inv, lows):
    size = gram[0].shape[0]
    at, start = divmod(offset, LANES)
    lane = lax.broadcasted_iota(jnp.int32, (size, LANES), 1)
    inside = jnp.logical_and(lane >= start, lane < start + size)
    if offset == 0:
        return None, None, jnp.where(inside, gram[0], 0.0)
    value = jnp.concatenate(gram, axis=1) if at else gram[0]
    low = matmul(value, inv, (1, 1))
    lows[offset:offset + size, :(at + 1) * LANES] = low
    square = matmul(low, lows[at * LANES:(at + 1) * LANES, :(at + 1) * LANES], (1, 1))
    return low, matmul(low, inv), jnp.where(inside, gram[at] - square, 0.0)


def triangles(done, start):
    lane = lax.broadcasted_iota(jnp.int32, done.shape, 1)
    row = start + lax.broadcasted_iota(jnp.int32, done.shape, 0)
    upper = jnp.where(lane >= row, done, 0.0)
    return upper, jnp.where(lane < row, done, jnp.where(lane == row, 1.0 / done, 0.0))


def pieces(both, hi_ref, lo_ref, keep):
    deep, pixels = both.shape[1], hi_ref.shape[1]
    tall = both.shape[0] // 2

    def piece(at):
        cut = slice(at, at + 2 * LANES)
        value = product(both, hi_ref[:deep, cut], (1, 0)) + product(both, lo_ref[:deep, cut], (1, 0))
        keep(at, value[:tall] + value[tall:])

    return [functools.partial(piece, at) for at in range(0, pixels, 2 * LANES)]


def spread_rows(out32, tile_rows, tall, at, value):
    for i in range(2):
        out32[pl.ds(at // LANES + i, tall, stride=tile_rows), :] = value[:tall, i * LANES:(i + 1) * LANES]


def smooth_rows(read, rows):
    decay = math.exp(-1.0 / 6.0)
    tail = math.exp(-(REACH + 1) / 6.0)
    ahead = read(0)
    for p in range(1, REACH + 1):
        ahead = ahead * decay + read(p)
    out = [ahead]
    for i in range(1, rows):
        ahead = ahead * decay + (read(REACH + i) - tail * read(i - 1))
        out.append(ahead)
    last = REACH + rows - 1
    back = read(last + REACH) * decay
    for k in range(REACH - 1, 0, -1):
        back = (back + read(last + k)) * decay
    out[rows - 1] = out[rows - 1] + back
    for i in range(rows - 2, -1, -1):
        p = REACH + i
        back = (back + read(p + 1)) * decay - tail * read(p + REACH + 1)
        out[i] = out[i] + back
    return out


def group_rows(exposures, group):
    part = exposures // CHUNKS
    return BOUNDS[group] * part, BOUNDS[group + 1] * part


def shares(exposures, total, group):
    first, stop = group_rows(exposures, group)
    tall = (stop - first) * (first // LANES + 1)
    return tall, -(-tall // total)


def exchange_kernel(ccds, tiles, pixel_total, frame_hbm, mask_hbm, good_hbm, w_hbm,
                    hi_ref, lo_ref, g_ref, x_ref, f_ref, early_ref,
                    good_ref, w_ref, frames, masks, flat, own, halo, done, lows, rows_ref, out32, *rest):
    bufs = [rest[3 * g:3 * g + 3] for g in range(GROUPS)]
    fs, ms, ws, hs, hr, s1, r1, s2, r2, ready = rest[3 * GROUPS:]
    exposures, tile_rows, h = frames.shape
    c, t = lax.axis_index("ccd"), lax.axis_index("tile")
    me, total = c * tiles + t, ccds * tiles
    after, before = lax.rem(me + 1, total), lax.rem(me + total - 1, total)
    after_id = (lax.div(after, tiles), lax.rem(after, tiles))
    before_id = (lax.div(before, tiles), lax.rem(before, tiles))
    part = exposures // CHUNKS
    span = part * tile_rows
    scale = 1.0 / pixel_total
    loads = []
    small = [pltpu.make_async_copy(good_hbm, good_ref, ws.at[0]), pltpu.make_async_copy(w_hbm, w_ref, ws.at[1])]
    small[0].start()
    for k in range(CHUNKS):
        block = pl.ds(k * part, part)
        pair = (pltpu.make_async_copy(frame_hbm.at[block], frames.at[block], fs.at[k]),
                pltpu.make_async_copy(mask_hbm.at[block], masks.at[block], ms.at[k]))
        for copy in pair:
            copy.start()
        loads.append(pair)
    small[1].start()
    barrier = pltpu.get_barrier_semaphore()
    for peer in (before_id, after_id):
        pl.semaphore_signal(barrier, inc=1, device_id=peer, device_id_type=MESH)
    for d in range(1, tiles):
        pl.semaphore_signal(barrier, inc=1, device_id=(c, lax.rem(t + d, tiles)), device_id_type=MESH)
    for d in range(1, ccds):
        pl.semaphore_signal(barrier, inc=1, device_id=(lax.rem(c + d, ccds), t), device_id_type=MESH)
    small[0].wait()
    good = good_ref[...].astype(jnp.float32)[None]

    def mask(k):
        block = pl.ds(k * part, part)
        for copy in loads[k]:
            copy.wait()
        value = frames[block].astype(jnp.float32) * (masks[block].astype(jnp.float32) * good)
        flat[k % 2] = value.reshape(span, h)
        for r in range(tile_rows):
            own[k, r] = flat[k % 2, pl.ds(r, part, stride=tile_rows), :].astype(jnp.bfloat16)

    moves = []

    def send(k):
        pair = []
        for side, peer in enumerate((after_id, before_id)):
            copy = pltpu.make_async_remote_copy(
                src_ref=own.at[k], dst_ref=halo.at[side, k], send_sem=hs.at[side, k],
                recv_sem=hr.at[side, k], device_id=peer, device_id_type=MESH)
            copy.start()
            pair.append(copy)
        moves.append(pair)

    mask(0)
    pl.semaphore_wait(barrier, tiles + ccds)
    send(0)
    for d in range(1, ccds):
        pl.semaphore_signal(ready, inc=1, device_id=(lax.rem(c + d, ccds), t), device_id_type=MESH)
    for k in range(1, CHUNKS):
        mask(k)
        if k < AHEAD:
            send(k)
    x_ref[...] = jnp.zeros(x_ref.shape, jnp.float32)
    f_ref[...] = jnp.zeros(f_ref.shape, jnp.float32)
    lows[...] = jnp.zeros(lows.shape, jnp.float32)
    for g in range(GROUPS):
        bufs[g][0][...] = jnp.zeros(bufs[g][0].shape, jnp.float32)
        first, stop = group_rows(exposures, g)
        left = LANES - stop % LANES
        if first % LANES == 0 and left < LANES:
            for ref in (hi_ref, lo_ref):
                ref[stop:stop + left, :] = jnp.zeros((left, ref.shape[1]), jnp.bfloat16)
    has_before = jnp.where(me > 0, 1.0, 0.0)
    has_after = jnp.where(me < total - 1, 1.0, 0.0)
    small[1].wait()
    weights = w_ref[...]
    step = 16

    def smooth(k):
        @pl.loop(0, part // step)
        def _(n):
            some = pl.ds(pl.multiple_of(n * step, step), step)

            def read(p):
                if p < tile_rows:
                    return halo[0, k, p, some, :].astype(jnp.float32) * has_before
                if p < 2 * tile_rows:
                    return own[k, p - tile_rows, some, :].astype(jnp.float32)
                return halo[1, k, p - 2 * tile_rows, some, :].astype(jnp.float32) * has_after

            for r, value in enumerate(smooth_rows(read, tile_rows)):
                high, low = split(value)
                where = pl.ds(pl.multiple_of(r * part + n * step, step), step)
                done[where, :h] = high
                done[where, h:] = low

        value = product(done[...], weights, (1, 0))
        high, low = split(value[:, :h] + value[:, h:])
        rows = slice(k * part, (k + 1) * part)
        for r in range(tile_rows):
            hi_ref[rows, r * h:(r + 1) * h] = high[r * part:(r + 1) * part]
            lo_ref[rows, r * h:(r + 1) * h] = low[r * part:(r + 1) * part]

    stages = {}

    def every(body):
        if total <= 64:
            for d in range(1, total):
                body(d)
        else:
            pl.loop(1, total)(body)

    def move(g, stage, src, dst, peer):
        send_sem, recv_sem = ((s1, r1), (s2, r2))[stage]
        return pltpu.make_async_remote_copy(
            src_ref=src, dst_ref=dst, send_sem=send_sem.at[g], recv_sem=recv_sem.at[g],
            device_id=(lax.div(peer, tiles), lax.rem(peer, tiles)), device_id_type=MESH)

    def all_of(g, stage):
        ref = bufs[g][1 + stage].at[pl.ds(0, total - 1)]
        return move(g, stage, ref, ref, after)

    def launch(g, stage):
        mine, near, whole = bufs[g]

        def body(d):
            peer = lax.rem(me + d, total)
            if stage == 0:
                move(g, 0, mine.at[peer], near.at[d - 1], peer).start()
            else:
                move(g, 1, whole.at[me], whole.at[me], peer).start()

        every(body)
        stages[g] = stage

    def gram(g):
        first, stop = group_rows(exposures, g)
        size = stop - first
        wide = (first // LANES + 1) * LANES
        some = jnp.concatenate([hi_ref[first:stop, :], lo_ref[first:stop, :]], axis=0)
        value = product(some, hi_ref[:wide, :], (1, 1)) + product(some, lo_ref[:wide, :], (1, 1))
        value = value[:size] + value[size:]
        packed = jnp.concatenate([value[:, w:w + LANES] for w in range(0, wide, LANES)], axis=0)
        mine = bufs[g][0]
        share = mine.shape[1]
        if g == 0:
            pl.semaphore_wait(ready, ccds - 1)
        for i in range(packed.shape[0] // share):
            mine[i] = packed[i * share:(i + 1) * share]
        launch(g, 0)

    def advance(g):
        mine, near, whole = bufs[g]
        all_of(g, stages[g]).wait_recv()
        if stages[g] == 0:
            parts = [mine[me]] + [near[i] for i in range(total - 1)] if total <= 64 else [mine[me] + jnp.sum(near[:total - 1], axis=0)]
            while len(parts) > 1:
                parts = [a + b for a, b in zip(parts[::2], parts[1::2])] + parts[len(parts) // 2 * 2:]
            whole[me] = parts[0]
            launch(g, 1)

    def gathered(g, ref):
        whole = bufs[g][2]
        tall, share = shares(exposures, total, g)
        for i in range(tall // share):
            ref[i * share:(i + 1) * share, :] = whole[i]
        return tall

    def basis(g):
        first, stop = group_rows(exposures, g)
        both = jnp.concatenate(split(x_ref[first:stop, :(first // LANES + 1) * LANES]), axis=0)
        return pieces(both, hi_ref, lo_ref, functools.partial(spread_rows, out32, tile_rows, stop - first))

    def keep(g):
        first, stop = group_rows(exposures, g)
        early_ref[first * tile_rows:stop * tile_rows, :] = out32[:(stop - first) * tile_rows, :].astype(jnp.bfloat16)

    def factor(g):
        value = flat[0, :gathered(g, flat.at[0]), :] * scale
        first, stop = group_rows(exposures, g)
        size, rows = stop - first, slice(first, stop)
        at, start = divmod(first, LANES)
        tiles_in = [value[w * size:(w + 1) * size] for w in range(at + 1)]
        low, spread, block = panel(tiles_in, first, x_ref[:(at + 1) * LANES, :(at + 1) * LANES], lows)
        lane = lax.broadcasted_iota(jnp.int32, block.shape, 1)
        live = [block if low is None else jnp.where(lane < start, -spread[:, at * LANES:], block)]
        if at:
            live = [-spread[:, w * LANES:(w + 1) * LANES] for w in range(at)] + live
        beside = BESIDE.get(g)
        eliminate(live, first, rows_ref, () if beside is None else basis(beside))
        cut = slice(at * LANES, (at + 1) * LANES)
        upper, lower = triangles(rows_ref[:size, cut], start)
        x_ref[rows, cut] = lower
        f_ref[rows, cut] = upper if low is None else jnp.where(lane < start, low[:, cut], upper)
        if at:
            x_ref[rows, :at * LANES] = rows_ref[:size, :at * LANES]
            f_ref[rows, :at * LANES] = low[:, :at * LANES]
        if beside is not None:
            keep(beside)
        if g in BEHIND:
            for piece in basis(g):
                piece()
            keep(g)

    for k in range(CHUNKS):
        for copy in moves[k]:
            copy.wait_recv()
        for g in SLOTS.get(k, ()):
            advance(g)
        smooth(k)
        if k + 1 in BOUNDS:
            gram(BOUNDS.index(k + 1) - 1)
        if k + AHEAD < CHUNKS:
            send(k + AHEAD)
        if k == FIRST:
            factor(0)
    for order, g in TAIL:
        for i in order:
            advance(i)
        if g is not None:
            factor(g)
    gathered(GROUPS - 1, g_ref)
    for g in range(GROUPS):
        for stage in range(2):
            all_of(g, stage).wait_send()
    for copy in sum(moves, []):
        copy.wait_send()


def exchange(frames, source_mask, good_pixels, weights, pixel_total):
    ccds, tiles = lax.axis_size("ccd"), lax.axis_size("tile")
    exposures, tile_rows, _ = frames.shape
    pixels = tile_rows * LANES
    part = exposures // CHUNKS
    span = part * tile_rows
    size = max(stop - first for first, stop in (group_rows(exposures, g) for g in range(GROUPS)))
    early = group_rows(exposures, GROUPS - 2)[0]
    dma = pltpu.SemaphoreType.DMA
    vm = pl.BlockSpec(memory_space=pltpu.VMEM)
    hbm = pl.BlockSpec(memory_space=pl.ANY)
    split_shape = pltpu.VMEM((exposures, pixels), jnp.bfloat16)
    square = pltpu.VMEM((exposures, exposures), jnp.float32)
    share = [shares(exposures, ccds * tiles, g) for g in range(GROUPS)]
    reduce = []
    for g in range(GROUPS):
        reduce += [pltpu.VMEM((ccds * tiles, share[g][1], LANES), jnp.float32)] * 3
    return pl.pallas_call(
        functools.partial(exchange_kernel, ccds, tiles, pixel_total),
        out_shape=(split_shape, split_shape, pltpu.VMEM((share[-1][0], LANES), jnp.float32), square, square,
                   pltpu.VMEM((early * tile_rows, LANES), jnp.bfloat16)),
        in_specs=[hbm] * 4,
        out_specs=(vm,) * 6,
        scratch_shapes=[
            pltpu.VMEM(good_pixels.shape, jnp.int32),
            pltpu.VMEM(weights.shape, jnp.bfloat16),
            pltpu.VMEM(frames.shape, jnp.bfloat16),
            pltpu.VMEM(frames.shape, jnp.int32),
            pltpu.VMEM((2, span, LANES), jnp.float32),
            pltpu.VMEM((CHUNKS, tile_rows, part, LANES), jnp.bfloat16),
            pltpu.VMEM((2, CHUNKS, tile_rows, part, LANES), jnp.bfloat16),
            pltpu.VMEM((span, 2 * LANES), jnp.bfloat16),
            pltpu.VMEM((exposures, exposures), jnp.float32),
            pltpu.VMEM((size, exposures), jnp.float32),
            pltpu.VMEM((size * tile_rows, LANES), jnp.float32),
            *reduce,
            dma((CHUNKS,)), dma((CHUNKS,)), dma((2,)),
            dma((2, CHUNKS)), dma((2, CHUNKS)),
            dma((GROUPS,)), dma((GROUPS,)), dma((GROUPS,)), dma((GROUPS,)),
            pltpu.SemaphoreType.REGULAR,
        ],
        compiler_params=pltpu.CompilerParams(collective_id=0, has_side_effects=True, vmem_limit_bytes=VMEM),
    )(*(pltpu.with_memory_space_constraint(x, pltpu.HBM) for x in (frames, source_mask, good_pixels, weights)))


def solve_kernel(pixel_total, g_ref, x_ref, f_ref, early_ref, hi_ref, lo_ref, o_hbm, b_hbm,
                 lows, rows_ref, out32, packed, rest_hi, rest_lo, factor, sems):
    exposures, pixels = hi_ref.shape
    tile_rows = pixels // LANES
    before, first = group_rows(exposures, GROUPS - 2)
    size, prior = exposures - first, first - before
    at, start = divmod(first, LANES)
    copies = []

    def out(src, dst):
        copy = pltpu.make_async_copy(src, dst, sems.at[len(copies)])
        copy.start()
        copies.append(copy)

    out(early_ref, b_hbm.at[pl.ds(0, early_ref.shape[0])])
    lows[...] = jnp.zeros(lows.shape, jnp.float32)
    value = g_ref[...] * (1.0 / pixel_total)
    low, spread, block = panel([value[w * size:(w + 1) * size] for w in range(at + 1)], first, x_ref[...], lows)
    row = first + lax.broadcasted_iota(jnp.int32, (size, exposures), 0)
    col = lax.broadcasted_iota(jnp.int32, (size, exposures), 1)
    rest = jnp.where(col < first, -spread, jnp.where(col == row, 1.0, 0.0))
    xh, xl = split(x_ref[before:first, :])
    rh, rl = split(rest)
    both = jnp.concatenate([xh, rh, xl, rl], axis=0)

    def keep(cut, value):
        spread_rows(out32, tile_rows, prior, cut, value)
        high, small = split(value[prior:])
        rest_hi[:, cut:cut + 2 * LANES] = high
        rest_lo[:, cut:cut + 2 * LANES] = small

    def rows_out(top, stop):
        tall = (stop - top) * tile_rows
        here = pl.ds((top - before) * tile_rows, tall)
        packed[here, :] = out32[:tall, :].astype(jnp.bfloat16)
        out(packed.at[here], b_hbm.at[pl.ds(top * tile_rows, tall)])

    def upper_rows():
        whole = jnp.concatenate([f_ref[:first, :], jnp.where(col < first, low, 0.0)], axis=0)
        down = lax.broadcasted_iota(jnp.int32, (exposures, exposures), 0)
        over = lax.broadcasted_iota(jnp.int32, (exposures, exposures), 1)
        same = over < 0
        for g in range(GROUPS - 1):
            a, b = group_rows(exposures, g)
            ranges = [jnp.logical_and(i >= a, i < b) for i in (down, over)]
            same = jnp.logical_or(same, jnp.logical_and(*ranges))
        both_sides = jnp.where(same, whole, 0.0) + jnp.where(jnp.logical_or(same, over > down), 0.0, whole).T
        factor[:first, :] = both_sides[:first]
        out(factor.at[pl.ds(0, first)], o_hbm.at[pl.ds(0, first)])

    fill = [upper_rows] + pieces(both, hi_ref, lo_ref, keep)
    eliminate([block], start, rows_ref, fill)
    upper, lower = triangles(rows_ref[...], start)
    rows_out(before, first)
    if at:
        factor[first:, :at * LANES] = jnp.zeros((size, at * LANES), jnp.float32)
    factor[first:, at * LANES:] = upper
    out(factor.at[pl.ds(first, size)], o_hbm.at[pl.ds(first, size)])
    both = jnp.concatenate(split(lower[:, start:start + size]), axis=0)
    for piece in pieces(both, rest_hi, rest_lo, functools.partial(spread_rows, out32, tile_rows, size)):
        piece()
    rows_out(first, exposures)
    for copy in copies:
        copy.wait()


def solve(gram, x, f, early, hi, lo, pixel_total):
    exposures, pixels = hi.shape
    before, first = group_rows(exposures, GROUPS - 2)
    size, tile_rows = exposures - first, pixels // LANES
    vm = pl.BlockSpec(memory_space=pltpu.VMEM)
    hbm = pl.BlockSpec(memory_space=pl.ANY)
    square = (exposures, exposures)
    rows = (exposures * pixels // LANES, LANES)
    given = (pltpu.with_memory_space_constraint(value, pltpu.VMEM) for value in (gram, x, f, early, hi, lo))
    return pl.pallas_call(
        functools.partial(solve_kernel, pixel_total),
        out_shape=(jax.ShapeDtypeStruct(square, jnp.float32), jax.ShapeDtypeStruct(rows, jnp.bfloat16)),
        in_specs=[vm] * 6,
        out_specs=(hbm, hbm),
        scratch_shapes=[
            pltpu.VMEM(square, jnp.float32),
            pltpu.VMEM((size, LANES), jnp.float32),
            pltpu.VMEM((max(size, first - before) * tile_rows, LANES), jnp.float32),
            pltpu.VMEM(((exposures - before) * tile_rows, LANES), jnp.bfloat16),
            pltpu.VMEM((size, pixels), jnp.bfloat16),
            pltpu.VMEM((size, pixels), jnp.bfloat16),
            pltpu.VMEM(square, jnp.float32),
            pltpu.SemaphoreType.DMA((5,)),
        ],
        compiler_params=pltpu.CompilerParams(vmem_limit_bytes=VMEM),
    )(*given)


def per_device(frames, source_mask, good_pixels):
    exposures, tile_rows, tile_cols = frames.shape
    tiles = lax.axis_size("tile")
    pixel_total = float(tile_rows * tile_cols * lax.axis_size("ccd") * tiles)
    hi, lo, gram, x, f, early = exchange(frames, source_mask, good_pixels, column_matrix(tile_cols), pixel_total)
    factor, basis = solve(gram, x, f, early, hi, lo, pixel_total)
    return (factor, basis.reshape(exposures, tile_rows, tile_cols))


def solution(mesh):
    in_specs = (
        P(None, ("ccd", "tile"), None),
        P(None, ("ccd", "tile"), None),
        P(("ccd", "tile"), None),
    )
    out_specs = (P(), P(None, ("ccd", "tile"), None))
    return jax.shard_map(
        per_device, mesh=mesh, in_specs=in_specs, out_specs=out_specs, check_vma=False
    )
```
